128 devices in a mesh: slab: 32 (over z, x, core), energy: 4 (over y).
Axes of the slice: x: 4, y: 4, z: 4, core: 2. Of those that a mesh axis runs over, the one named last changes fastest.
Arguments:
- onsite: float32 [64, 2, 256, 256], P('slab'), as said below
- hop: float32 [64, 2, 256, 256], P('slab'), may hold values from -0.1875 to 0.1875
- energy_level: float32 [4], P('energy'), parts along dimension 0, may hold values from -0.5 to 0.5
- broadening: float32 [4], P('energy'), parts along dimension 0, may hold values from 0.4 to 0.8
Outputs:
- diagonal: float32 [256, 2, 256, 256], P(('energy', 'slab')), parts along dimension 0
- upper: float32 [256, 2, 256, 256], P(('energy', 'slab')), parts along dimension 0
- lower: float32 [256, 2, 256, 256], P(('energy', 'slab')), parts along dimension 0
The draws below stay inside these ranges and needn't reach their ends.
There are 4 independent parts, one for each index of `energy`. The reference program is written for one: setup_inputs(seed, part) draws one part's arguments, and reference() takes and returns one part's arrays. A program takes and returns all parts, laid end to end along the dimension named above; an argument that names none is the same for every part. Nothing has to cross between parts.
Inputs may be any that keep to these rules, and one draw needn't show every extreme that they name: Each block of onsite is Hermitian: real part symmetric, imaginary part antisymmetric.
All inputs are finite; a program needn't handle non-finite values.
Results may differ from the reference program's by a relative error of at most 0.0003.
Values sent between devices are 32-bit elements; how exact they have to be, the bound alone decides.
No kernel may reach another device: no remote copies, remote signals or barrier semaphores. Data moves between devices by JAX's collectives and lax.ppermute only.
A program may use at most 128 MiB of HBM per device.

```python
import math
import jax
import jax.numpy as jnp
from jax import lax

B = 256
LEVELS = 3
NSLAB = 64


def draw_onsite(key, part):
    first, second = jax.random.split(key, 2)
    sigma = 0.4 / B ** 0.5
    real_draw = jax.random.normal(first, (NSLAB, B, B), jnp.float32) * sigma
    imag_draw = jax.random.normal(second, (NSLAB, B, B), jnp.float32) * sigma
    real_part = 0.5 * (real_draw + jnp.swapaxes(real_draw, 1, 2))
    imag_part = 0.5 * (imag_draw - jnp.swapaxes(imag_draw, 1, 2))
    return jnp.stack([real_part, imag_part], axis=1).astype(jnp.float32)


def level_of(rng, shape, cuts, low, top_value):
    gain, own = 1.0, jax.random.fold_in(rng, 6)
    for position, shards_of in cuts:
        heights = jnp.exp(jax.random.uniform(jax.random.fold_in(own, position), (shards_of,), jnp.float32, low / len(cuts), top_value / len(cuts)))
        gain = gain * jnp.repeat(heights, shape[position] // shards_of).reshape([-1 if axis == position else 1 for axis in range(len(shape))])
    return gain


def noise(own_key, extent, deviation, most, pieces=(), kind=jnp.bfloat16):
    entries = deviation * jax.random.normal(own_key, extent, jnp.float32)
    if pieces:
        entries = entries * level_of(own_key, extent, pieces, -0.22, 0.18)
    return jnp.clip(entries, -most, most).astype(kind)


def setup_inputs(seed: int = 0, part: int = 0) -> dict:
    key_of = jax.random.split(jax.random.key(seed), 5)
    part_splits = jax.random.split(jax.random.fold_in(key_of[4], part), 5)
    onsite = draw_onsite(jax.random.fold_in(key_of[4], 71), part)
    hop = noise(key_of[1], (NSLAB, 2, B, B), (0.5 / B ** 0.5), 0.1875, ((0, 32),), jnp.float32)
    energy_level = jnp.clip(jax.random.uniform(part_splits[2], (1,), jnp.float32, -0.5, 0.5), -0.5, 0.5)
    broadening = jnp.clip(jnp.exp(jax.random.uniform(part_splits[3], (1,), jnp.float32, math.log(0.4), math.log(0.8))), 0.4, 0.8)
    return dict(onsite=onsite, hop=hop, energy_level=energy_level, broadening=broadening)


highest = lax.Precision.HIGHEST

def complex_product(left, right):
    left_re = left[:, 0]
    left_im = left[:, 1]
    right_re = right[:, 0]
    right_im = right[:, 1]

    def multiply(first, second):
        return jnp.einsum('nij,njk->nik', first, second, precision=highest)
    real_part = multiply(left_re, right_re) - multiply(left_im, right_im)
    imag_part = multiply(left_re, right_im) + multiply(left_im, right_re)
    return jnp.stack([real_part, imag_part], axis=1)

def embedded(blocks):
    real_part = blocks[:, 0]
    imag_part = blocks[:, 1]
    top_half = jnp.concatenate([real_part, -imag_part], axis=2)
    bottom_half = jnp.concatenate([imag_part, real_part], axis=2)
    return jnp.concatenate([top_half, bottom_half], axis=1)

def split_halves(solved, width):
    return jnp.stack([solved[:, :width], solved[:, width:]], axis=1)

def from_lower(values, stride, slabs):
    padding = jnp.zeros((stride,) + values.shape[1:], jnp.float32)
    return jnp.concatenate([padding, values], axis=0)[:slabs]

def from_upper(values, stride, slabs):
    padding = jnp.zeros((stride,) + values.shape[1:], jnp.float32)
    return jnp.concatenate([values, padding], axis=0)[stride:stride + slabs]

def reference(onsite, hop, energy_level, broadening):
    slabs = onsite.shape[0]
    width = onsite.shape[2]
    identity = jnp.eye(width, dtype=jnp.float32)
    diagonal = jnp.stack([energy_level[0] * identity - onsite[:, 0], broadening[0] * identity - onsite[:, 1]], axis=1)
    keep = (jnp.arange(slabs) < slabs - 1).astype(jnp.float32)
    upper = -hop * keep[:, None, None, None]
    shifted = jnp.concatenate([jnp.zeros_like(hop[:1]), hop[:-1]], axis=0)
    lower = jnp.stack([-jnp.swapaxes(shifted[:, 0], 1, 2), jnp.swapaxes(shifted[:, 1], 1, 2)], axis=1)
    for level in range(LEVELS):
        stride = 2 ** level
        system = embedded(diagonal)
        targets = jnp.concatenate([jnp.concatenate([upper[:, 0], lower[:, 0]], axis=2), jnp.concatenate([upper[:, 1], lower[:, 1]], axis=2)], axis=1)
        solved = jnp.linalg.solve(system, targets)
        solved_up = split_halves(solved[:, :, :width], width)
        solved_low = split_halves(solved[:, :, width:], width)
        new_diagonal = diagonal - complex_product(lower, from_lower(solved_up, stride, slabs)) - complex_product(upper, from_upper(solved_low, stride, slabs))
        new_lower = -complex_product(lower, from_lower(solved_low, stride, slabs))
        new_upper = -complex_product(upper, from_upper(solved_up, stride, slabs))
        diagonal, lower, upper = (new_diagonal, new_lower, new_upper)
    return (diagonal, upper, lower)
```

```python
import functools

import jax
import jax.numpy as jnp
from jax import lax
from jax.experimental import pallas as pl
from jax.experimental.pallas import tpu as pltpu
from jax.sharding import PartitionSpec as P


BF = jnp.bfloat16
F32 = jnp.float32
HIGHEST = lax.Precision.HIGHEST
CONVERGED = 0.998
TRUSTED = 0.012
VMEM = pl.BlockSpec(memory_space=pltpu.VMEM)
SMEM = pl.BlockSpec(memory_space=pltpu.SMEM)


def dot(a, b):
    return jnp.dot(a, b, preferred_element_type=F32)


def exact_dot(a, b):
    return jnp.dot(a, b, precision=HIGHEST, preferred_element_type=F32)


def emb(c):
    w = c.shape[1]
    re, im = c[:w], c[w:]
    return jnp.concatenate(
        [jnp.concatenate([re, -im], axis=1), jnp.concatenate([im, re], axis=1)], axis=0
    )


def adjoint(c):
    w = c.shape[1]
    return jnp.concatenate([c[:w].T, -c[w:].T], axis=0)


def split(c):
    high = c.astype(BF)
    return high, (c - high.astype(F32)).astype(BF)


def product(a, b):
    a_high, a_low = split(a)
    b_high, b_low = split(b)
    e_high, e_low = emb(a_high), emb(a_low)
    return dot(e_high, b_high) + dot(e_high, b_low) + dot(e_low, b_high)


def unit(w):
    row = lax.broadcasted_iota(jnp.int32, (2 * w, w), 0)
    col = lax.broadcasted_iota(jnp.int32, (2 * w, w), 1)
    return (row == col).astype(F32)


def invert(blocks, eta, z, ea, el, cx):
    w = blocks[0].shape[1]
    one = unit(w)
    norms = []
    for i, a in enumerate(blocks):
        high, low = split(a)
        ea[i] = emb(high)
        el[i] = emb(low)
        ah = adjoint(a)
        gram = dot(ea[i], ah.astype(BF))
        size = jnp.sqrt(gram[:w] * gram[:w] + gram[w:] * gram[w:])
        norm = 1.02 * jnp.max(jnp.sum(size, axis=1))
        cx[i] = (ah * (1.0 / norm)).astype(BF)
        norms.append(norm)
    largest = functools.reduce(jnp.maximum, norms)
    start = jnp.maximum(0.9 * eta * eta / largest, 1e-10)

    def step(bound):
        mu = 2.0 / (bound + 1.03)
        for i in range(len(blocks)):
            x = cx[i]
            error = (one - mu * dot(ea[i], x)).astype(BF)
            cx[i] = (mu * (x.astype(F32) + dot(emb(x), error))).astype(BF)
        gap = 1.0 - mu * bound
        return 1.0 - gap * gap

    lax.while_loop(lambda bound: bound < CONVERGED, step, start)
    for i, a in enumerate(blocks):
        x = cx[i]
        error = one - (dot(ea[i], x) + dot(el[i], x))
        z[i] = x.astype(F32) + dot(emb(x), error.astype(BF))
        left = jnp.sum(error * error)

        @pl.when(jnp.logical_not(left <= TRUSTED))
        def _():
            full = emb(a)

            @pl.when(jnp.logical_not(left <= 0.25))
            def _():
                z[i] = adjoint(a) * (1.0 / norms[i])

            def polish(state):
                count, _ = state
                now = z[i]
                rest = one - exact_dot(full, now)
                z[i] = now + exact_dot(emb(now), rest)
                return count + 1, jnp.sum(rest * rest)

            lax.while_loop(
                lambda state: (state[0] < 64) & jnp.logical_not(state[1] <= 1e-6),
                polish,
                (0, jnp.float32(1.0)),
            )


def initial(onsite, scalars):
    w = onsite.shape[1]
    row = lax.broadcasted_iota(jnp.int32, (2 * w, w), 0)
    col = lax.broadcasted_iota(jnp.int32, (2 * w, w), 1)
    shift = jnp.where(row == col, scalars[0], jnp.where(row == col + w, scalars[1], 0.0))
    return shift - onsite


def solve(d, lower, upper, eta, payload, z, ea, el, cx):
    invert([d], eta, z, ea, el, cx)
    both = product(z[0], jnp.concatenate([upper, lower], axis=1))
    w = d.shape[1]
    payload[: 2 * w] = both[:, :w]
    payload[2 * w :] = both[:, w:]


def first_kernel(onsite, scalars, z_out, z, ea, el, cx):
    blocks = [initial(onsite[i], scalars) for i in range(onsite.shape[0])]
    invert(blocks, scalars[1], z, ea, el, cx)
    for i in range(len(blocks)):
        z_out[i] = z[i]


def second_kernel(
    onsite, h_m2, h_m1, h_0, h_p1, z_m, z_p, scalars, d_out, l_out, u_out, payload, z, ea, el, cx
):
    w = onsite.shape[1]
    h0 = h_0[...]
    t = product(product(h0, z_p[...]), jnp.concatenate([adjoint(h0), h_p1[...]], axis=1))
    d = initial(onsite[...], scalars) - t[:, :w]
    upper = t[:, w:] * (-scalars[2])
    hm = h_m1[...]
    t = product(product(adjoint(hm), z_m[...]), jnp.concatenate([hm, adjoint(h_m2[...])], axis=1))
    d = d - t[:, :w]
    lower = -t[:, w:]
    d_out[...] = d
    l_out[...] = lower
    u_out[...] = upper
    solve(d_out[...], lower, upper, scalars[1], payload, z, ea, el, cx)


def reduced(d, lower, upper, below, above):
    w = d.shape[1]
    from_below = product(lower, jnp.concatenate([below[: 2 * w], below[2 * w :]], axis=1))
    from_above = product(upper, jnp.concatenate([above[: 2 * w], above[2 * w :]], axis=1))
    return (
        d - from_below[:, :w] - from_above[:, w:],
        -from_below[:, w:],
        -from_above[:, :w],
    )


def third_kernel(
    d_in, l_in, u_in, below, above, scalars, d_out, l_out, u_out, payload, z, ea, el, cx
):
    d, lower, upper = reduced(d_in[...], l_in[...], u_in[...], below, above)
    d_out[...] = d
    l_out[...] = lower
    u_out[...] = upper
    solve(d_out[...], lower, upper, scalars[1], payload, z, ea, el, cx)


def last_kernel(d_in, l_in, u_in, below, above, d_out, u_out, l_out):
    d, lower, upper = reduced(d_in[...], l_in[...], u_in[...], below, above)
    d_out[0] = d
    l_out[0] = lower
    u_out[0] = upper


def last_kernel_beside(d_in, l_in, u_in, below, above, d_old, u_old, l_old, d_out, u_out, l_out):
    last_kernel(d_in, l_in, u_in, below, above, d_out, u_out, l_out)


def shape(*dims):
    return jax.ShapeDtypeStruct(dims, F32)


def work(count, w):
    return [
        pltpu.VMEM((count, 2 * w, w), F32),
        pltpu.VMEM((count, 2 * w, 2 * w), BF),
        pltpu.VMEM((count, 2 * w, 2 * w), BF),
        pltpu.VMEM((count, 2 * w, w), BF),
    ]


PARAMS = pltpu.CompilerParams(vmem_limit_bytes=24 << 20)


def send(x, by):
    size = lax.axis_size("slab")
    return lax.ppermute(x, "slab", [(i, i + by) for i in range(size) if 0 <= i + by < size])


def on_device(onsite, hop, energy_level, broadening):
    rows, _, w, _ = onsite.shape
    onsite = onsite.reshape(rows, 2 * w, w)
    hop = hop.reshape(rows, 2 * w, w)
    last = lax.axis_index("slab") == lax.axis_size("slab") - 1
    keep = jnp.where(last, 0.0, 1.0).astype(F32)
    scalars_a = jnp.stack([energy_level[0], broadening[0], keep])
    scalars_b = jnp.stack([energy_level[0], broadening[0], jnp.float32(1.0)])

    hop_left = send(hop, 1)
    hop_right = send(hop[0], -1)
    block = shape(2 * w, w)
    inverse = pl.pallas_call(
        first_kernel,
        out_shape=shape(rows, 2 * w, w),
        in_specs=[VMEM, SMEM],
        out_specs=VMEM,
        scratch_shapes=work(rows, w),
        compiler_params=PARAMS,
        name="first",
    )(onsite, scalars_a)
    z_left = send(inverse[1], 1)
    z_right = send(inverse[0], -1)

    second = pl.pallas_call(
        second_kernel,
        out_shape=(block, block, block, shape(4 * w, w)),
        in_specs=[VMEM] * 7 + [SMEM],
        out_specs=(VMEM,) * 4,
        scratch_shapes=work(1, w),
        compiler_params=PARAMS,
        name="second",
    )
    state_a = second(
        onsite[0], hop_left[0], hop_left[1], hop[0], hop[1], z_left, inverse[1], scalars_a
    )
    below_a, above_a = send(state_a[3], 1), send(state_a[3], -1)
    state_b = second(
        onsite[1], hop_left[1], hop[0], hop[1], hop_right, inverse[0], z_right, scalars_b
    )
    below_b, above_b = send(state_b[3], 1), send(state_b[3], -1)

    third = pl.pallas_call(
        third_kernel,
        out_shape=(block, block, block, shape(4 * w, w)),
        in_specs=[VMEM] * 5 + [SMEM],
        out_specs=(VMEM,) * 4,
        scratch_shapes=work(1, w),
        compiler_params=PARAMS,
        name="third",
    )
    state_a = third(*state_a[:3], below_a, above_a, scalars_a)
    below_a, above_a = send(state_a[3], 2), send(state_a[3], -2)
    state_b = third(*state_b[:3], below_b, above_b, scalars_a)
    below_b, above_b = send(state_b[3], 2), send(state_b[3], -2)

    def at(k):
        return (pl.BlockSpec((1, 2 * w, w), lambda i: (k, 0, 0)),) * 3

    whole = shape(rows, 2 * w, w)
    out = pl.pallas_call(
        last_kernel,
        grid=(1,),
        out_shape=(whole,) * 3,
        in_specs=[VMEM] * 5,
        out_specs=at(0),
        compiler_params=PARAMS,
        name="last",
    )(*state_a[:3], below_a, above_a)
    out = pl.pallas_call(
        last_kernel_beside,
        grid=(1,),
        out_shape=(whole,) * 3,
        in_specs=[VMEM] * 5 + [pl.BlockSpec(memory_space=pl.ANY)] * 3,
        out_specs=at(1),
        input_output_aliases={5: 0, 6: 1, 7: 2},
        compiler_params=PARAMS,
        name="last_beside",
    )(*state_b[:3], below_b, above_b, *out)
    return tuple(x.reshape(rows, 2, w, w) for x in out)


def solution(mesh):
    placed = (P("slab", None, None, None), P("slab", None, None, None), P("energy"), P("energy"))
    out = P(("energy", "slab"), None, None, None)
    return jax.shard_map(
        on_device, mesh=mesh, in_specs=placed, out_specs=(out, out, out), check_vma=False
    )
```

```python
import functools

import jax
import jax.numpy as jnp
from jax import lax
from jax.experimental import pallas as pl
from jax.experimental.pallas import tpu as pltpu
from jax.sharding import PartitionSpec as P


BF = jnp.bfloat16
F32 = jnp.float32
HIGHEST = lax.Precision.HIGHEST
CONVERGED = 0.998
TRUSTED = 0.012
VMEM = pl.BlockSpec(memory_space=pltpu.VMEM)
SMEM = pl.BlockSpec(memory_space=pltpu.SMEM)


def dot(a, b):
    return jnp.dot(a, b, preferred_element_type=F32)


def exact_dot(a, b):
    return jnp.dot(a, b, precision=HIGHEST, preferred_element_type=F32)


def row(c):
    w = c.shape[1]
    return jnp.concatenate([c[:w], c[w:]], axis=1)


def put(out, r, at=0):
    w = r.shape[0]
    out[at : at + w] = r[:, :w]
    out[at + w : at + 2 * w] = r[:, w:]


def turned(r):
    w = r.shape[1] // 2
    return jnp.concatenate([-r[:, w:], r[:, :w]], axis=1)


def emb(r):
    return jnp.concatenate([r, turned(r)], axis=0)


def adjoint(r):
    w = r.shape[0]
    return jnp.concatenate([r[:, :w].T, -r[:, w:].T], axis=1)


def split(x):
    high = x.astype(BF)
    return high, (x - high.astype(F32)).astype(BF)


def product(a, b):
    a_high, a_low = split(a)
    b_high, b_low = split(b)
    e_high, e_low = emb(b_high), emb(b_low)
    return dot(a_high, e_high) + dot(a_high, e_low) + dot(a_low, e_high)


def unit(w):
    at = lax.broadcasted_iota(jnp.int32, (w, 2 * w), 0)
    return (at == lax.broadcasted_iota(jnp.int32, (w, 2 * w), 1)).astype(F32)


def invert(blocks, eta, work, side=()):
    z, ea, el, ex, full, spread, rest = work
    w = blocks[0].shape[0]
    one = unit(w)
    halves = [slice(k * w // 2, (k + 1) * w // 2) for k in range(2)]

    def place(i, x):
        ex[i, :w] = x
        ex[i, w:] = turned(x)

    norms = []
    for i, a in enumerate(blocks):
        high, low = split(a)
        ea[i] = emb(high)
        el[i] = emb(low)
        ah = adjoint(high)
        gram = dot(ah, ea[i])
        size = jnp.sqrt(gram[:, :w] * gram[:, :w] + gram[:, w:] * gram[:, w:])
        norm = 1.02 * jnp.max(jnp.sum(size, axis=1))
        place(i, (ah.astype(F32) * (1.0 / norm)).astype(BF))
        norms.append(norm)
    largest = functools.reduce(jnp.maximum, norms)
    bound = jnp.maximum(0.9 * eta * eta / largest, 1e-10)

    def step(bound, piece=None):
        mu = 2.0 / (bound + 1.03)
        for i in range(len(blocks)):
            errors = [(one[h] - mu * dot(ex[i, h], ea[i])).astype(BF) for h in halves]
            if piece is not None:
                piece()
            news = [
                (mu * (ex[i, h].astype(F32) + dot(e, ex[i]))).astype(BF)
                for h, e in zip(halves, errors)
            ]
            place(i, jnp.concatenate(news, axis=0))
        gap = 1.0 - mu * bound
        return 1.0 - gap * gap

    for piece in side:
        bound = step(bound, piece)
    lax.while_loop(lambda bound: bound < CONVERGED, step, bound)
    for i, a in enumerate(blocks):
        x = ex[i, :w]
        error = one - (dot(x, ea[i]) + dot(x, el[i]))
        z[i] = x.astype(F32) + dot(error.astype(BF), ex[i])
        left = jnp.sum(error * error)

        @pl.when(jnp.logical_not(left <= TRUSTED))
        def _():
            polish(a, norms[i], left, z, i, full, spread, rest)


def polish(a, norm, left, z, i, full, spread, rest):
    w = a.shape[0]
    high, wide = min(64, w), min(128, w)
    across = 2 * w // wide
    full[...] = emb(a)

    @pl.when(jnp.logical_not(left <= 0.25))
    def _():
        z[i] = adjoint(a) * (1.0 / norm)

    def cut(k):
        top, side = k // across * high, k % across * wide
        return (
            top,
            side,
            pl.ds(pl.multiple_of(top, high), high),
            pl.ds(pl.multiple_of(side, wide), wide),
        )

    def once(state):
        def residual(k, total):
            top, side, rows, cols = cut(k)
            at = lax.broadcasted_iota(jnp.int32, (high, wide), 0) + top
            to = lax.broadcasted_iota(jnp.int32, (high, wide), 1) + side
            part = jnp.where(at == to, 1.0, 0.0) - exact_dot(z[i, rows, :], full[:, cols])
            rest[rows, cols] = part
            return total + jnp.sum(part * part)

        tiles = w // high * across
        total = lax.fori_loop(0, tiles, residual, jnp.float32(0.0))
        spread[...] = emb(z[i])

        def correct(k, _):
            _, _, rows, cols = cut(k)
            z[i, rows, cols] += exact_dot(rest[rows, :], spread[:, cols])
            return 0

        lax.fori_loop(0, tiles, correct, 0)
        return state[0] + 1, total

    lax.while_loop(
        lambda state: (state[0] < 64) & jnp.logical_not(state[1] <= 1e-6),
        once,
        (0, jnp.float32(1.0)),
    )


def initial(onsite, scalars):
    w = onsite.shape[0]
    at = lax.broadcasted_iota(jnp.int32, (w, 2 * w), 0)
    to = lax.broadcasted_iota(jnp.int32, (w, 2 * w), 1)
    shift = jnp.where(at == to, scalars[0], jnp.where(at + w == to, scalars[1], 0.0))
    return shift - onsite


def deferred(out, a, b, sign):
    a_high, a_low = split(a)
    b_high, b_low = split(b)

    def lead():
        put(out, sign * dot(a_high, emb(b_high)))

    def middle():
        put(out, row(out[...]) + sign * dot(a_high, emb(b_low)))

    def trail():
        put(out, row(out[...]) + sign * dot(a_low, emb(b_high)))

    return lead, middle, trail


def paired(first, second):
    def piece():
        first()
        second()

    return piece


def solve(d, lower, upper, side, eta, payload, work):
    invert([d], eta, work, side)
    z = work[0][0]
    put(payload, product(z, row(upper[...])))
    put(payload, product(z, row(lower[...])), upper.shape[0])


def first_kernel(onsite, hop, scalars, up, down, sem, *work):
    w = onsite.shape[2]
    beside = pltpu.make_async_copy(hop.at[0], down.at[pl.ds(2 * w, 2 * w)], sem)
    beside.start()
    invert([initial(row(onsite[i]), scalars) for i in range(2)], scalars[1], work)
    put(up, work[0][1])
    put(down, work[0][0])
    beside.wait()


def second_kernel(
    onsite, h_m2, h_m1, h_0, h_p1, z_m, z_p, scalars, d_out, l_out, u_out, payload, *work
):
    h0, hm = row(h_0[...]), row(h_m1[...])
    from_above = product(h0, row(z_p[...]))
    from_below = product(adjoint(hm), row(z_m[...]))
    d = (
        initial(row(onsite[...]), scalars)
        - product(from_above, adjoint(h0))
        - product(from_below, hm)
    )
    put(d_out, d)
    set_upper = deferred(u_out, from_above, row(h_p1[...]), -scalars[2])
    set_lower = deferred(l_out, from_below, adjoint(row(h_m2[...])), -1.0)
    side = [paired(*pair) for pair in zip(set_upper, set_lower)]
    solve(row(d_out[...]), l_out, u_out, side, scalars[1], payload, work)


def third_kernel(
    d_in, l_in, u_in, below, above, scalars, d_out, l_out, u_out, payload, *work
):
    w = d_in.shape[1]
    lower, upper = row(l_in[...]), row(u_in[...])
    d = (
        row(d_in[...])
        - product(lower, row(below[: 2 * w]))
        - product(upper, row(above[2 * w :]))
    )
    put(d_out, d)
    set_upper = deferred(u_out, upper, row(above[: 2 * w]), -1.0)
    set_lower = deferred(l_out, lower, row(below[2 * w :]), -1.0)
    side = [paired(*pair) for pair in zip(set_upper, set_lower)]
    solve(row(d_out[...]), l_out, u_out, side, scalars[1], payload, work)


def last_kernel(d_in, l_in, u_in, below, above, d_out, u_out, l_out):
    w = d_in.shape[1]
    lower, upper = row(l_in[...]), row(u_in[...])
    d = (
        row(d_in[...])
        - product(lower, row(below[: 2 * w]))
        - product(upper, row(above[2 * w :]))
    )
    put(d_out.at[0], d)
    put(l_out.at[0], -product(lower, row(below[2 * w :])))
    put(u_out.at[0], -product(upper, row(above[: 2 * w])))


def last_below(d_in, l_in, below, l_old, d_mid, l_out):
    w = d_in.shape[1]
    lower = row(l_in[...])
    put(d_mid, row(d_in[...]) - product(lower, row(below[: 2 * w])))
    put(l_out.at[0], -product(lower, row(below[2 * w :])))


def last_above(d_mid, u_in, above, d_old, u_old, d_out, u_out):
    w = d_mid.shape[1]
    upper = row(u_in[...])
    put(d_out.at[0], row(d_mid[...]) - product(upper, row(above[2 * w :])))
    put(u_out.at[0], -product(upper, row(above[: 2 * w])))


def shape(*dims):
    return jax.ShapeDtypeStruct(dims, F32)


def work(count, w):
    return [
        pltpu.VMEM((count, w, 2 * w), F32),
        pltpu.VMEM((count, 2 * w, 2 * w), BF),
        pltpu.VMEM((count, 2 * w, 2 * w), BF),
        pltpu.VMEM((count, 2 * w, 2 * w), BF),
        pltpu.VMEM((2 * w, 2 * w), F32),
        pltpu.VMEM((2 * w, 2 * w), F32),
        pltpu.VMEM((w, 2 * w), F32),
    ]


PARAMS = pltpu.CompilerParams(vmem_limit_bytes=24 << 20)


def send(x, by):
    size = lax.axis_size("slab")
    return lax.ppermute(x, "slab", [(i, i + by) for i in range(size) if 0 <= i + by < size])


def reduce_levels(onsite, hop, energy_level, broadening):
    rows, _, w, _ = onsite.shape
    onsite = onsite.reshape(rows, 2 * w, w)
    hop = hop.reshape(rows, 2 * w, w)
    last = lax.axis_index("slab") == lax.axis_size("slab") - 1
    keep = jnp.where(last, 0.0, 1.0).astype(F32)
    scalars_a = jnp.stack([energy_level[0], broadening[0], keep])
    scalars_b = jnp.stack([energy_level[0], broadening[0], jnp.float32(1.0)])

    hop_left = send(hop, 1)
    block = shape(2 * w, w)
    inverse_b, inverse_hop_a = pl.pallas_call(
        first_kernel,
        out_shape=(block, shape(4 * w, w)),
        in_specs=[VMEM, pl.BlockSpec(memory_space=pltpu.HBM), SMEM],
        out_specs=(VMEM, VMEM),
        scratch_shapes=[pltpu.SemaphoreType.DMA] + work(rows, w),
        compiler_params=PARAMS,
        name="first",
    )(onsite, hop, scalars_a)
    z_left = send(inverse_b, 1)
    z_hop_right = send(inverse_hop_a, -1)
    inverse_a = inverse_hop_a[: 2 * w]
    z_right, hop_right = z_hop_right[: 2 * w], z_hop_right[2 * w :]

    second = pl.pallas_call(
        second_kernel,
        out_shape=(block, block, block, shape(4 * w, w)),
        in_specs=[VMEM] * 7 + [SMEM],
        out_specs=(VMEM,) * 4,
        scratch_shapes=work(1, w),
        compiler_params=PARAMS,
        name="second",
    )
    state_a = second(
        onsite[0], hop_left[0], hop_left[1], hop[0], hop[1], z_left, inverse_b, scalars_a
    )
    below_a, above_a = send(state_a[3], 1), send(state_a[3], -1)
    state_b = second(
        onsite[1], hop_left[1], hop[0], hop[1], hop_right, inverse_a, z_right, scalars_b
    )
    below_b, above_b = send(state_b[3], 1), send(state_b[3], -1)

    third = pl.pallas_call(
        third_kernel,
        out_shape=(block, block, block, shape(4 * w, w)),
        in_specs=[VMEM] * 5 + [SMEM],
        out_specs=(VMEM,) * 4,
        scratch_shapes=work(1, w),
        compiler_params=PARAMS,
        name="third",
    )
    state_a = third(*state_a[:3], below_a, above_a, scalars_a)
    below_a, above_a = send(state_a[3], 2), send(state_a[3], -2)
    state_b = third(*state_b[:3], below_b, above_b, scalars_a)
    below_b, above_b = send(state_b[3], 2), send(state_b[3], -2)

    def at(k):
        return pl.BlockSpec((1, 2 * w, w), lambda i: (k, 0, 0))

    whole = shape(rows, 2 * w, w)
    kept = pl.BlockSpec(memory_space=pl.ANY)
    d_out, u_out, l_out = pl.pallas_call(
        last_kernel,
        grid=(1,),
        out_shape=(whole,) * 3,
        in_specs=[VMEM] * 5,
        out_specs=(at(0),) * 3,
        compiler_params=PARAMS,
        name="last",
    )(*state_a[:3], below_a, above_a)
    d, lower, upper = state_b[:3]
    d, l_out = pl.pallas_call(
        last_below,
        grid=(1,),
        out_shape=(block, whole),
        in_specs=[VMEM] * 3 + [kept],
        out_specs=(VMEM, at(1)),
        input_output_aliases={3: 1},
        compiler_params=PARAMS,
        name="last_below",
    )(d, lower, below_b, l_out)
    d_out, u_out = pl.pallas_call(
        last_above,
        grid=(1,),
        out_shape=(whole, whole),
        in_specs=[VMEM] * 3 + [kept] * 2,
        out_specs=(at(1), at(1)),
        input_output_aliases={3: 0, 4: 1},
        compiler_params=PARAMS,
        name="last_above",
    )(d, upper, above_b, d_out, u_out)
    return tuple(x.reshape(rows, 2, w, w) for x in (d_out, u_out, l_out))


def solution(mesh):
    placed = (P("slab", None, None, None), P("slab", None, None, None), P("energy"), P("energy"))
    out = P(("energy", "slab"), None, None, None)
    return jax.shard_map(
        reduce_levels, mesh=mesh, in_specs=placed, out_specs=(out, out, out), check_vma=False
    )
```

```python
import functools

import jax
import jax.numpy as jnp
from jax import lax
from jax.experimental import pallas as pl
from jax.experimental.pallas import tpu as pltpu
from jax.sharding import PartitionSpec as P


BF = jnp.bfloat16
F32 = jnp.float32
HIGHEST = lax.Precision.HIGHEST
CONVERGED = 0.998
TRUSTED = 0.012
VMEM = pl.BlockSpec(memory_space=pltpu.VMEM)
SMEM = pl.BlockSpec(memory_space=pltpu.SMEM)


def dot(a, b):
    return jnp.dot(a, b, preferred_element_type=F32)


def exact_dot(a, b):
    return jnp.dot(a, b, precision=HIGHEST, preferred_element_type=F32)


def row(c):
    w = c.shape[1]
    return jnp.concatenate([c[:w], c[w:]], axis=1)


def put(out, r, at=0):
    w = r.shape[0]
    out[at : at + w] = r[:, :w]
    out[at + w : at + 2 * w] = r[:, w:]


def turned(r):
    w = r.shape[1] // 2
    return jnp.concatenate([-r[:, w:], r[:, :w]], axis=1)


def emb(r):
    return jnp.concatenate([r, turned(r)], axis=0)


def adjoint(r):
    w = r.shape[0]
    return jnp.concatenate([r[:, :w].T, -r[:, w:].T], axis=1)


def split(x):
    high = x.astype(BF)
    return high, (x - high.astype(F32)).astype(BF)


def product(a, b):
    a_high, a_low = split(a)
    b_high, b_low = split(b)
    e_high, e_low = emb(b_high), emb(b_low)
    return dot(a_high, e_high) + dot(a_high, e_low) + dot(a_low, e_high)


def unit(w):
    at = lax.broadcasted_iota(jnp.int32, (w, 2 * w), 0)
    return (at == lax.broadcasted_iota(jnp.int32, (w, 2 * w), 1)).astype(F32)


def invert(blocks, eta, work, side=()):
    z, ea, el, ex, full, spread, rest = work
    w = blocks[0].shape[0]
    one = unit(w)
    halves = [slice(k * w // 2, (k + 1) * w // 2) for k in range(2)]

    def place(i, x):
        ex[i, :w] = x
        ex[i, w:] = turned(x)

    norms = []
    for i, a in enumerate(blocks):
        high, low = split(a)
        ea[i] = emb(high)
        el[i] = emb(low)
        ah = adjoint(high)
        gram = dot(ah, ea[i])
        size = jnp.sqrt(gram[:, :w] * gram[:, :w] + gram[:, w:] * gram[:, w:])
        norm = 1.02 * jnp.max(jnp.sum(size, axis=1))
        place(i, (ah.astype(F32) * (1.0 / norm)).astype(BF))
        norms.append(norm)
    largest = functools.reduce(jnp.maximum, norms)
    bound = jnp.maximum(0.9 * eta * eta / largest, 1e-10)

    def step(bound, piece=None):
        mu = 2.0 / (bound + 1.03)
        for i in range(len(blocks)):
            errors = [(one[h] - mu * dot(ex[i, h], ea[i])).astype(BF) for h in halves]
            if piece is not None:
                piece()
            news = [
                (mu * (ex[i, h].astype(F32) + dot(e, ex[i]))).astype(BF)
                for h, e in zip(halves, errors)
            ]
            place(i, jnp.concatenate(news, axis=0))
        gap = 1.0 - mu * bound
        return 1.0 - gap * gap

    for piece in side:
        bound = step(bound, piece)
    lax.while_loop(lambda bound: bound < CONVERGED, step, bound)
    for i, a in enumerate(blocks):
        x = ex[i, :w]
        error = one - (dot(x, ea[i]) + dot(x, el[i]))
        z[i] = x.astype(F32) + dot(error.astype(BF), ex[i])
        left = jnp.sum(error * error)

        @pl.when(jnp.logical_not(left <= TRUSTED))
        def _():
            polish(a, norms[i], left, z, i, full, spread, rest)


def polish(a, norm, left, z, i, full, spread, rest):
    w = a.shape[0]
    high, wide = min(64, w), min(128, w)
    across = 2 * w // wide
    full[...] = emb(a)

    @pl.when(jnp.logical_not(left <= 0.25))
    def _():
        z[i] = adjoint(a) * (1.0 / norm)

    def cut(k):
        top, side = k // across * high, k % across * wide
        return (
            top,
            side,
            pl.ds(pl.multiple_of(top, high), high),
            pl.ds(pl.multiple_of(side, wide), wide),
        )

    def once(state):
        def residual(k, total):
            top, side, rows, cols = cut(k)
            at = lax.broadcasted_iota(jnp.int32, (high, wide), 0) + top
            to = lax.broadcasted_iota(jnp.int32, (high, wide), 1) + side
            part = jnp.where(at == to, 1.0, 0.0) - exact_dot(z[i, rows, :], full[:, cols])
            rest[rows, cols] = part
            return total + jnp.sum(part * part)

        tiles = w // high * across
        total = lax.fori_loop(0, tiles, residual, jnp.float32(0.0))
        spread[...] = emb(z[i])

        def correct(k, _):
            _, _, rows, cols = cut(k)
            z[i, rows, cols] += exact_dot(rest[rows, :], spread[:, cols])
            return 0

        lax.fori_loop(0, tiles, correct, 0)
        return state[0] + 1, total

    lax.while_loop(
        lambda state: (state[0] < 64) & jnp.logical_not(state[1] <= 1e-6),
        once,
        (0, jnp.float32(1.0)),
    )


def initial(onsite, scalars):
    w = onsite.shape[0]
    at = lax.broadcasted_iota(jnp.int32, (w, 2 * w), 0)
    to = lax.broadcasted_iota(jnp.int32, (w, 2 * w), 1)
    shift = jnp.where(at == to, scalars[0], jnp.where(at + w == to, scalars[1], 0.0))
    return shift - onsite


def deferred(out, k, a, b, sign):
    a_high, a_low = split(a)
    b_high, b_low = split(b)

    def lead():
        put(out.at[k], sign * dot(a_high, emb(b_high)))

    def middle():
        put(out.at[k], row(out[k]) + sign * dot(a_high, emb(b_low)))

    def trail():
        put(out.at[k], row(out[k]) + sign * dot(a_low, emb(b_high)))

    return lead, middle, trail


def paired(first, second):
    def piece():
        first()
        second()

    return piece


def solve(d, couplings, side, eta, payload, work):
    invert([d], eta, work, side)
    z = work[0][0]
    for k in range(2):
        put(payload.at[k], product(z, row(couplings[1 - k])))


def sides(parity):
    return 1 - parity, parity


def first_kernel(onsite, hop, scalars, up, down, sem, *work):
    w = onsite.shape[2]
    beside = pltpu.make_async_copy(hop.at[0], down.at[pl.ds(2 * w, 2 * w)], sem)
    beside.start()
    invert([initial(row(onsite[i]), scalars) for i in range(2)], scalars[1], work)
    put(up, work[0][1])
    put(down, work[0][0])
    beside.wait()


def second_kernel(
    onsite, h_m2, h_m1, h_0, h_p1, z_m, z_p, scalars, d_out, c_out, payload, *work
):
    h0, hm = row(h_0[...]), row(h_m1[...])
    from_above = product(h0, row(z_p[...]))
    from_below = product(adjoint(hm), row(z_m[...]))
    d = (
        initial(row(onsite[...]), scalars)
        - product(from_above, adjoint(h0))
        - product(from_below, hm)
    )
    put(d_out, d)
    set_upper = deferred(c_out, 1, from_above, row(h_p1[...]), -scalars[2])
    set_lower = deferred(c_out, 0, from_below, adjoint(row(h_m2[...])), -1.0)
    side = [paired(*pair) for pair in zip(set_upper, set_lower)]
    solve(row(d_out[...]), c_out, side, scalars[1], payload, work)


def third_kernel(d_in, c_in, even, odd, scalars, parity, d_out, c_out, payload, *work):
    i, j = sides(parity[0])
    one, two = row(c_in[i]), row(c_in[j])
    d = row(d_in[...]) - product(one, row(even[i])) - product(two, row(odd[j]))
    put(d_out, d)
    set_one = deferred(c_out, i, one, row(even[1 - i]), -1.0)
    set_two = deferred(c_out, j, two, row(odd[1 - j]), -1.0)
    side = [paired(*pair) for pair in zip(set_one, set_two)]
    solve(row(d_out[...]), c_out, side, scalars[1], payload, work)


def last_odd(d_in, c_in, odd, parity, d_mid, c_mid):
    _, j = sides(parity[1])
    two = row(c_in[j])
    put(d_mid, row(d_in[...]) - product(two, row(odd[j])))
    put(c_mid, -product(two, row(odd[1 - j])))


def last_even(d_mid, c_mid, c_in, even, parity, d_out, u_out, l_out):
    i, _ = sides(parity[1])
    one = row(c_in[i])
    put(d_out.at[0], row(d_mid[...]) - product(one, row(even[i])))
    mine, other = -product(one, row(even[1 - i])), row(c_mid[...])
    put(u_out.at[0], jnp.where(i == 1, mine, other))
    put(l_out.at[0], jnp.where(i == 1, other, mine))


def last_even_beside(
    d_mid, c_mid, c_in, even, parity, d_old, u_old, l_old, d_out, u_out, l_out
):
    last_even(d_mid, c_mid, c_in, even, parity, d_out, u_out, l_out)


def shape(*dims):
    return jax.ShapeDtypeStruct(dims, F32)


def work(count, w):
    return [
        pltpu.VMEM((count, w, 2 * w), F32),
        pltpu.VMEM((count, 2 * w, 2 * w), BF),
        pltpu.VMEM((count, 2 * w, 2 * w), BF),
        pltpu.VMEM((count, 2 * w, 2 * w), BF),
        pltpu.VMEM((2 * w, 2 * w), F32),
        pltpu.VMEM((2 * w, 2 * w), F32),
        pltpu.VMEM((w, 2 * w), F32),
    ]


PARAMS = pltpu.CompilerParams(vmem_limit_bytes=20 << 20)


def send(x, by):
    size = lax.axis_size("slab")
    return lax.ppermute(x, "slab", [(i, i + by) for i in range(size) if 0 <= i + by < size])


def swaps(x, by):
    size = lax.axis_size("slab")
    even, odd = [], []
    for i in range(size - by):
        pairs = odd if i // by % 2 else even
        pairs += [(i, i + by), (i + by, i)]
    from_odd = lax.ppermute(x, "slab", odd)
    from_even = lax.ppermute(x, "slab", even)
    return from_even, from_odd


def reduce_levels(onsite, hop, energy_level, broadening):
    rows, _, w, _ = onsite.shape
    onsite = onsite.reshape(rows, 2 * w, w)
    hop = hop.reshape(rows, 2 * w, w)
    last = lax.axis_index("slab") == lax.axis_size("slab") - 1
    keep = jnp.where(last, 0.0, 1.0).astype(F32)
    scalars_a = jnp.stack([energy_level[0], broadening[0], keep])
    scalars_b = jnp.stack([energy_level[0], broadening[0], jnp.float32(1.0)])

    hop_left = send(hop, 1)
    block = shape(2 * w, w)
    inverse_b, inverse_hop_a = pl.pallas_call(
        first_kernel,
        out_shape=(block, shape(4 * w, w)),
        in_specs=[VMEM, pl.BlockSpec(memory_space=pltpu.HBM), SMEM],
        out_specs=(VMEM, VMEM),
        scratch_shapes=[pltpu.SemaphoreType.DMA] + work(rows, w),
        compiler_params=PARAMS,
        name="first",
    )(onsite, hop, scalars_a)
    z_left = send(inverse_b, 1)
    z_hop_right = send(inverse_hop_a, -1)
    inverse_a = inverse_hop_a[: 2 * w]
    z_right, hop_right = z_hop_right[: 2 * w], z_hop_right[2 * w :]

    position = lax.axis_index("slab")
    parity = jnp.stack([position % 2, position // 2 % 2]).astype(jnp.int32)
    two = shape(2, 2 * w, w)
    second = pl.pallas_call(
        second_kernel,
        out_shape=(block, two, two),
        in_specs=[VMEM] * 7 + [SMEM],
        out_specs=(VMEM,) * 3,
        scratch_shapes=work(1, w),
        compiler_params=PARAMS,
        name="second",
    )
    d_a, c_a, p_a = second(
        onsite[0], hop_left[0], hop_left[1], hop[0], hop[1], z_left, inverse_b, scalars_a
    )
    even_a, odd_a = swaps(p_a, 1)
    d_b, c_b, p_b = second(
        onsite[1], hop_left[1], hop[0], hop[1], hop_right, inverse_a, z_right, scalars_b
    )
    even_b, odd_b = swaps(p_b, 1)

    third = pl.pallas_call(
        third_kernel,
        out_shape=(block, two, two),
        in_specs=[VMEM] * 4 + [SMEM] * 2,
        out_specs=(VMEM,) * 3,
        scratch_shapes=work(1, w),
        compiler_params=PARAMS,
        name="third",
    )
    d_a, c_a, p_a = third(d_a, c_a, even_a, odd_a, scalars_a, parity)
    even_a, odd_a = swaps(p_a, 2)
    d_b, c_b, p_b = third(d_b, c_b, even_b, odd_b, scalars_a, parity)
    even_b, odd_b = swaps(p_b, 2)

    def at(k):
        return (pl.BlockSpec((1, 2 * w, w), lambda i: (k, 0, 0)),) * 3

    whole = shape(rows, 2 * w, w)
    half = pl.pallas_call(
        last_odd,
        out_shape=(block, block),
        in_specs=[VMEM] * 3 + [SMEM],
        out_specs=(VMEM,) * 2,
        compiler_params=PARAMS,
        name="last_odd",
    )
    d_a, o_a = half(d_a, c_a, odd_a, parity)
    out = pl.pallas_call(
        last_even,
        grid=(1,),
        out_shape=(whole,) * 3,
        in_specs=[VMEM] * 4 + [SMEM],
        out_specs=at(0),
        compiler_params=PARAMS,
        name="last_even",
    )(d_a, o_a, c_a, even_a, parity)
    d_b, o_b = half(d_b, c_b, odd_b, parity)
    out = pl.pallas_call(
        last_even_beside,
        grid=(1,),
        out_shape=(whole,) * 3,
        in_specs=[VMEM] * 4 + [SMEM] + [pl.BlockSpec(memory_space=pl.ANY)] * 3,
        out_specs=at(1),
        input_output_aliases={5: 0, 6: 1, 7: 2},
        compiler_params=PARAMS,
        name="last_even_beside",
    )(d_b, o_b, c_b, even_b, parity, *out)
    return tuple(x.reshape(rows, 2, w, w) for x in out)


def solution(mesh):
    placed = (P("slab", None, None, None), P("slab", None, None, None), P("energy"), P("energy"))
    out = P(("energy", "slab"), None, None, None)
    return jax.shard_map(
        reduce_levels, mesh=mesh, in_specs=placed, out_specs=(out, out, out), check_vma=False
    )
```

```python
import functools

import jax
import jax.numpy as jnp
from jax import lax
from jax.experimental import pallas as pl
from jax.experimental.pallas import tpu as pltpu
from jax.sharding import PartitionSpec as P


BF = jnp.bfloat16
F32 = jnp.float32
HIGHEST = lax.Precision.HIGHEST
CONVERGED = 0.985
TRUSTED = 0.012
VMEM = pl.BlockSpec(memory_space=pltpu.VMEM)
SMEM = pl.BlockSpec(memory_space=pltpu.SMEM)


def dot(a, b):
    return jnp.dot(a, b, preferred_element_type=F32)


def exact_dot(a, b):
    return jnp.dot(a, b, precision=HIGHEST, preferred_element_type=F32)


def row(c):
    w = c.shape[1]
    return jnp.concatenate([c[:w], c[w:]], axis=1)


def put(out, r, at=0):
    w = r.shape[0]
    out[at : at + w] = r[:, :w]
    out[at + w : at + 2 * w] = r[:, w:]


def turned(r):
    w = r.shape[1] // 2
    return jnp.concatenate([-r[:, w:], r[:, :w]], axis=1)


def emb(r):
    return jnp.concatenate([r, turned(r)], axis=0)


def adjoint(r):
    w = r.shape[0]
    return jnp.concatenate([r[:, :w].T, -r[:, w:].T], axis=1)


def split(x):
    high = x.astype(BF)
    return high, (x - high.astype(F32)).astype(BF)


def product(a, b):
    a_high, a_low = split(a)
    b_high, b_low = split(b)
    e_high, e_low = emb(b_high), emb(b_low)
    return dot(a_high, e_high) + dot(a_high, e_low) + dot(a_low, e_high)


def unit(w):
    at = lax.broadcasted_iota(jnp.int32, (w, 2 * w), 0)
    return (at == lax.broadcasted_iota(jnp.int32, (w, 2 * w), 1)).astype(F32)


def invert(blocks, eta, work, side=()):
    z, ea, el, ex, full, spread, rest = work
    w = blocks[0].shape[0]
    one = unit(w)
    halves = [slice(k * w // 2, (k + 1) * w // 2) for k in range(2)]

    def place(i, x):
        ex[i, :w] = x
        ex[i, w:] = turned(x)

    norms = []
    for i, a in enumerate(blocks):
        high, low = split(a)
        ea[i] = emb(high)
        el[i] = emb(low)
        ah = adjoint(high)
        gram = dot(ah, ea[i])
        size = jnp.sqrt(gram[:, :w] * gram[:, :w] + gram[:, w:] * gram[:, w:])
        norm = 1.02 * jnp.max(jnp.sum(size, axis=1))
        place(i, (ah.astype(F32) * (1.0 / norm)).astype(BF))
        norms.append(norm)
    largest = functools.reduce(jnp.maximum, norms)
    bound = jnp.maximum(0.9 * eta * eta / largest, 1e-10)

    def step(bound, piece=None):
        mu = 2.0 / (bound + 1.03)
        for i in range(len(blocks)):
            errors = [(one[h] - mu * dot(ex[i, h], ea[i])).astype(BF) for h in halves]
            if piece is not None:
                piece()
            news = [
                (mu * (ex[i, h].astype(F32) + dot(e, ex[i]))).astype(BF)
                for h, e in zip(halves, errors)
            ]
            place(i, jnp.concatenate(news, axis=0))
        gap = 1.0 - mu * bound
        return 1.0 - gap * gap

    for piece in side:
        bound = step(bound, piece)
    lax.while_loop(lambda bound: bound < CONVERGED, step, bound)
    for i, a in enumerate(blocks):
        x = ex[i, :w]
        error = one - (dot(x, ea[i]) + dot(x, el[i]))
        z[i] = x.astype(F32) + dot(error.astype(BF), ex[i])
        left = jnp.sum(error * error)

        @pl.when(jnp.logical_not(left <= TRUSTED))
        def _():
            polish(a, norms[i], left, z, i, full, spread, rest)


def polish(a, norm, left, z, i, full, spread, rest):
    w = a.shape[0]
    high, wide = min(64, w), min(128, w)
    across = 2 * w // wide
    full[...] = emb(a)

    @pl.when(jnp.logical_not(left <= 0.25))
    def _():
        z[i] = adjoint(a) * (1.0 / norm)

    def cut(k):
        top, side = k // across * high, k % across * wide
        return (
            top,
            side,
            pl.ds(pl.multiple_of(top, high), high),
            pl.ds(pl.multiple_of(side, wide), wide),
        )

    def once(state):
        def residual(k, total):
            top, side, rows, cols = cut(k)
            at = lax.broadcasted_iota(jnp.int32, (high, wide), 0) + top
            to = lax.broadcasted_iota(jnp.int32, (high, wide), 1) + side
            part = jnp.where(at == to, 1.0, 0.0) - exact_dot(z[i, rows, :], full[:, cols])
            rest[rows, cols] = part
            return total + jnp.sum(part * part)

        tiles = w // high * across
        total = lax.fori_loop(0, tiles, residual, jnp.float32(0.0))
        spread[...] = emb(z[i])

        def correct(k, _):
            _, _, rows, cols = cut(k)
            z[i, rows, cols] += exact_dot(rest[rows, :], spread[:, cols])
            return 0

        lax.fori_loop(0, tiles, correct, 0)
        return state[0] + 1, total

    lax.while_loop(
        lambda state: (state[0] < 64) & jnp.logical_not(state[1] <= 1e-6),
        once,
        (0, jnp.float32(1.0)),
    )


def initial(onsite, scalars):
    w = onsite.shape[0]
    at = lax.broadcasted_iota(jnp.int32, (w, 2 * w), 0)
    to = lax.broadcasted_iota(jnp.int32, (w, 2 * w), 1)
    shift = jnp.where(at == to, scalars[0], jnp.where(at + w == to, scalars[1], 0.0))
    return shift - onsite


def deferred(out, k, a, b, sign):
    a_high, a_low = split(a)
    b_high, b_low = split(b)

    def lead():
        put(out.at[k], sign * dot(a_high, emb(b_high)))

    def middle():
        put(out.at[k], row(out[k]) + sign * dot(a_high, emb(b_low)))

    def trail():
        put(out.at[k], row(out[k]) + sign * dot(a_low, emb(b_high)))

    return lead, middle, trail


def paired(first, second):
    def piece():
        first()
        second()

    return piece


def solve(d, couplings, side, eta, payload, work):
    invert([d], eta, work, side)
    z = work[0][0]
    for k in range(2):
        put(payload, product(z, row(couplings[1 - k])), k * d.shape[1])


def part(payload, k):
    rows = 2 * payload.shape[1]
    return row(payload[pl.ds(pl.multiple_of(k * rows, rows), rows)])


def sides(parity):
    return 1 - parity, parity


def first_kernel(onsite, hop, scalars, up, down, sem, *work):
    w = onsite.shape[2]
    beside = pltpu.make_async_copy(hop.at[0], down.at[pl.ds(2 * w, 2 * w)], sem)
    beside.start()
    invert([initial(row(onsite[i]), scalars) for i in range(2)], scalars[1], work)
    put(up, work[0][1])
    put(down, work[0][0])
    beside.wait()


def near_kernel(onsite, hop, hop_left, z_b, z_hop_a, scalars, d_a, d_b, u_a, l_b, g_a, k_a):
    h = row(hop[0])
    before = row(hop_left[1])
    put(g_a, adjoint(before))
    put(k_a, adjoint(row(hop_left[0])))
    t = product(h, row(z_b[...]))
    put(d_a, initial(row(onsite[0]), scalars) - product(t, adjoint(h)))
    put(u_a, product(t, row(hop[1])) * (-scalars[2]))
    t = product(adjoint(h), part(z_hop_a, 0))
    put(d_b, initial(row(onsite[1]), scalars) - product(t, h))
    put(l_b, -product(t, adjoint(before)))


def second_kernel(d_in, c_in, g, z, k, scalars, side, d_out, c_out, payload, *work):
    at = side[0]
    gain = row(g[...])
    t = product(gain, row(z[...]))
    put(d_out, row(d_in[...]) - product(t, adjoint(gain)))
    c_out[1 - at] = c_in[...]
    pieces = deferred(c_out, at, t, row(k[...]), -1.0)
    solve(row(d_out[...]), c_out, pieces, scalars[1], payload, work)


def third_kernel(d_in, c_in, even, odd, scalars, parity, d_out, c_out, payload, *work):
    i, j = sides(parity[0])
    one, two = row(c_in[i]), row(c_in[j])
    d = row(d_in[...]) - product(one, part(even, i)) - product(two, part(odd, j))
    put(d_out, d)
    set_one = deferred(c_out, i, one, part(even, 1 - i), -1.0)
    set_two = deferred(c_out, j, two, part(odd, 1 - j), -1.0)
    side = [paired(*pair) for pair in zip(set_one, set_two)]
    solve(row(d_out[...]), c_out, side, scalars[1], payload, work)


def last_odd(d_in, c_in, odd, parity, d_mid, c_mid):
    _, j = sides(parity[1])
    two = row(c_in[j])
    put(d_mid, row(d_in[...]) - product(two, part(odd, j)))
    put(c_mid, -product(two, part(odd, 1 - j)))


def last_even(slab, d_mid, c_mid, c_in, even, parity, d_out, u_out, l_out, hold, sems):
    i, _ = sides(parity[1])
    one = row(c_in[i])
    mine, other = -product(one, part(even, 1 - i)), row(c_mid[...])
    copies = [
        pltpu.make_async_copy(hold.at[k], out.at[slab], sems.at[k])
        for k, out in enumerate((u_out, l_out, d_out))
    ]
    put(hold.at[0], jnp.where(i == 1, mine, other))
    put(hold.at[1], jnp.where(i == 1, other, mine))
    copies[0].start()
    copies[1].start()
    put(hold.at[2], row(d_mid[...]) - product(one, part(even, i)))
    copies[2].start()
    for copy in copies:
        copy.wait()


def last_even_beside(
    d_mid, c_mid, c_in, even, parity, d_old, u_old, l_old, d_out, u_out, l_out, hold, sems
):
    last_even(1, d_mid, c_mid, c_in, even, parity, d_out, u_out, l_out, hold, sems)


def shape(*dims):
    return jax.ShapeDtypeStruct(dims, F32)


def work(count, w):
    return [
        pltpu.VMEM((count, w, 2 * w), F32),
        pltpu.VMEM((count, 2 * w, 2 * w), BF),
        pltpu.VMEM((count, 2 * w, 2 * w), BF),
        pltpu.VMEM((count, 2 * w, 2 * w), BF),
        pltpu.VMEM((2 * w, 2 * w), F32),
        pltpu.VMEM((2 * w, 2 * w), F32),
        pltpu.VMEM((w, 2 * w), F32),
    ]


PARAMS = pltpu.CompilerParams(vmem_limit_bytes=20 << 20)


def send(x, by):
    size = lax.axis_size("slab")
    return lax.ppermute(x, "slab", [(i, i + by) for i in range(size) if 0 <= i + by < size])


def swaps(x, by):
    size = lax.axis_size("slab")
    even, odd = [], []
    for i in range(size - by):
        pairs = odd if i // by % 2 else even
        pairs += [(i, i + by), (i + by, i)]
    from_odd = lax.ppermute(x, "slab", odd)
    from_even = lax.ppermute(x, "slab", even)
    return from_even, from_odd


def reduce_levels(onsite, hop, energy_level, broadening):
    rows, _, w, _ = onsite.shape
    onsite = onsite.reshape(rows, 2 * w, w)
    hop = hop.reshape(rows, 2 * w, w)
    last = lax.axis_index("slab") == lax.axis_size("slab") - 1
    keep = jnp.where(last, 0.0, 1.0).astype(F32)
    scalars = jnp.stack([energy_level[0], broadening[0], keep])
    position = lax.axis_index("slab")
    parity = jnp.stack([position & 1, (position >> 1) & 1])
    scalars, parity = lax.optimization_barrier((scalars, parity))

    hop_left = send(hop, 1)
    block, pair, two = shape(2 * w, w), shape(4 * w, w), shape(2, 2 * w, w)
    up, down = pl.pallas_call(
        first_kernel,
        out_shape=(block, pair),
        in_specs=[VMEM, pl.BlockSpec(memory_space=pl.ANY), SMEM],
        out_specs=(VMEM,) * 2,
        scratch_shapes=[pltpu.SemaphoreType.DMA] + work(rows, w),
        compiler_params=PARAMS,
        name="first",
    )(onsite, pltpu.with_memory_space_constraint(hop, pltpu.HBM), scalars)
    z_left = send(up, 1)
    z_hop_right = send(down, -1)
    d_a, d_b, u_a, l_b, g_a, k_a = pl.pallas_call(
        near_kernel,
        out_shape=(block,) * 6,
        in_specs=[VMEM] * 5 + [SMEM],
        out_specs=(VMEM,) * 6,
        compiler_params=PARAMS,
        name="near",
    )(onsite, hop, hop_left, up, down, scalars)

    second = pl.pallas_call(
        second_kernel,
        out_shape=(block, two, pair),
        in_specs=[VMEM] * 5 + [SMEM] * 2,
        out_specs=(VMEM,) * 3,
        scratch_shapes=work(1, w),
        compiler_params=PARAMS,
        name="second",
    )
    d_a, c_a, p_a = second(d_a, u_a, g_a, z_left, k_a, scalars, jnp.zeros((1,), jnp.int32))
    even_a, odd_a = swaps(p_a, 1)
    d_b, c_b, p_b = second(
        d_b,
        l_b,
        hop[1],
        z_hop_right[: 2 * w],
        z_hop_right[2 * w :],
        scalars,
        jnp.ones((1,), jnp.int32),
    )
    even_b, odd_b = swaps(p_b, 1)

    third = pl.pallas_call(
        third_kernel,
        out_shape=(block, two, pair),
        in_specs=[VMEM] * 4 + [SMEM] * 2,
        out_specs=(VMEM,) * 3,
        scratch_shapes=work(1, w),
        compiler_params=PARAMS,
        name="third",
    )
    d_a, c_a, p_a = third(d_a, c_a, even_a, odd_a, scalars, parity)
    even_a, odd_a = swaps(p_a, 2)
    d_b, c_b, p_b = third(d_b, c_b, even_b, odd_b, scalars, parity)
    even_b, odd_b = swaps(p_b, 2)

    whole = shape(rows, 2 * w, w)
    kept = pl.BlockSpec(memory_space=pl.ANY)
    hold = [pltpu.VMEM((3, 2 * w, w), F32), pltpu.SemaphoreType.DMA((3,))]
    half = pl.pallas_call(
        last_odd,
        out_shape=(block, block),
        in_specs=[VMEM] * 3 + [SMEM],
        out_specs=(VMEM,) * 2,
        compiler_params=PARAMS,
        name="last_odd",
    )
    d_a, o_a = half(d_a, c_a, odd_a, parity)
    first_half = pl.pallas_call(
        functools.partial(last_even, 0),
        out_shape=(whole,) * 3,
        in_specs=[VMEM] * 4 + [SMEM],
        out_specs=(kept,) * 3,
        scratch_shapes=hold,
        compiler_params=PARAMS,
        name="last_even",
    )
    out = first_half(d_a, o_a, c_a, even_a, parity)
    d_b, o_b = half(d_b, c_b, odd_b, parity)
    out = pl.pallas_call(
        last_even_beside,
        out_shape=(whole,) * 3,
        in_specs=[VMEM] * 4 + [SMEM] + [kept] * 3,
        out_specs=(kept,) * 3,
        input_output_aliases={5: 0, 6: 1, 7: 2},
        scratch_shapes=hold,
        compiler_params=PARAMS,
        name="last_even_beside",
    )(d_b, o_b, c_b, even_b, parity, *out)
    return tuple(x.reshape(rows, 2, w, w) for x in out)


def solution(mesh):
    placed = (P("slab", None, None, None), P("slab", None, None, None), P("energy"), P("energy"))
    out = P(("energy", "slab"), None, None, None)
    return jax.shard_map(
        reduce_levels, mesh=mesh, in_specs=placed, out_specs=(out, out, out), check_vma=False
    )
```

```python
import functools

import jax
import jax.numpy as jnp
from jax import lax
from jax.experimental import pallas as pl
from jax.experimental.pallas import tpu as pltpu
from jax.sharding import PartitionSpec as P


BF = jnp.bfloat16
F32 = jnp.float32
HIGHEST = lax.Precision.HIGHEST
CONVERGED = 0.985
TRUSTED = 0.012
VMEM = pl.BlockSpec(memory_space=pltpu.VMEM)
SMEM = pl.BlockSpec(memory_space=pltpu.SMEM)


def dot(a, b):
    return jnp.dot(a, b, preferred_element_type=F32)


def exact_dot(a, b):
    return jnp.dot(a, b, precision=HIGHEST, preferred_element_type=F32)


def row(c):
    w = c.shape[1]
    return jnp.concatenate([c[:w], c[w:]], axis=1)


def put(out, r, at=0):
    w = r.shape[0]
    out[at : at + w] = r[:, :w]
    out[at + w : at + 2 * w] = r[:, w:]


def turned(r):
    w = r.shape[1] // 2
    return jnp.concatenate([-r[:, w:], r[:, :w]], axis=1)


def emb(r):
    return jnp.concatenate([r, turned(r)], axis=0)


def adjoint(r):
    w = r.shape[0]
    return jnp.concatenate([r[:, :w].T, -r[:, w:].T], axis=1)


def split(x):
    high = x.astype(BF)
    return high, (x - high.astype(F32)).astype(BF)


def product(a, b):
    return times(split(a), b)


def times(a, b):
    a_high, a_low = a
    b_high, b_low = split(b)
    e_high, e_low = emb(b_high), emb(b_low)
    return dot(a_high, e_high) + dot(a_high, e_low) + dot(a_low, e_high)


def unit(w):
    at = lax.broadcasted_iota(jnp.int32, (w, 2 * w), 0)
    return (at == lax.broadcasted_iota(jnp.int32, (w, 2 * w), 1)).astype(F32)


def invert(blocks, eta, work, side=()):
    z, ea, el, ex, full, spread, rest = work
    w = blocks[0].shape[0]
    one = unit(w)
    halves = [slice(k * w // 2, (k + 1) * w // 2) for k in range(2)]

    def place(i, x):
        ex[i, :w] = x
        ex[i, w:] = turned(x)

    norms, grams = [], []
    for i, a in enumerate(blocks):
        high, low = split(a)
        ea[i] = emb(high)
        el[i] = emb(low)
        ah = adjoint(high)
        gram = dot(ah, ea[i])
        size = jnp.sqrt(gram[:, :w] * gram[:, :w] + gram[:, w:] * gram[:, w:])
        norm = 1.02 * jnp.max(jnp.sum(size, axis=1))
        place(i, (ah.astype(F32) * (1.0 / norm)).astype(BF))
        norms.append(norm)
        grams.append(gram)
    largest = functools.reduce(jnp.maximum, norms)
    bound = jnp.maximum(0.9 * eta * eta / largest, 1e-10)

    def step(bound, piece=None, known=None):
        mu = 2.0 / (bound + 1.03)
        for i in range(len(blocks)):
            if known is None:
                errors = [(one[h] - mu * dot(ex[i, h], ea[i])).astype(BF) for h in halves]
            else:
                errors = [(one[h] - (mu / norms[i]) * known[i][h]).astype(BF) for h in halves]
            if piece is not None:
                piece()
            news = [
                (mu * (ex[i, h].astype(F32) + dot(e, ex[i]))).astype(BF)
                for h, e in zip(halves, errors)
            ]
            place(i, jnp.concatenate(news, axis=0))
        gap = 1.0 - mu * bound
        return 1.0 - gap * gap

    bound = step(bound, side[0] if side else None, grams)
    for piece in side[1:]:
        bound = step(bound, piece)
    lax.while_loop(lambda bound: bound < CONVERGED, step, bound)
    for i, a in enumerate(blocks):
        x = ex[i, :w]
        error = one - (dot(x, ea[i]) + dot(x, el[i]))
        z[i] = x.astype(F32) + dot(error.astype(BF), ex[i])
        left = jnp.sum(error * error)

        @pl.when(jnp.logical_not(left <= TRUSTED))
        def _():
            polish(a, norms[i], left, z, i, full, spread, rest)


def polish(a, norm, left, z, i, full, spread, rest):
    w = a.shape[0]
    high, wide = min(32, w), min(128, w)
    across = 2 * w // wide
    full[...] = emb(a)

    @pl.when(jnp.logical_not(left <= 0.25))
    def _():
        z[i] = adjoint(a) * (1.0 / norm)

    def cut(k):
        top, side = k // across * high, k % across * wide
        return (
            top,
            side,
            pl.ds(pl.multiple_of(top, high), high),
            pl.ds(pl.multiple_of(side, wide), wide),
        )

    def once(state):
        def residual(k, total):
            top, side, rows, cols = cut(k)
            at = lax.broadcasted_iota(jnp.int32, (high, wide), 0) + top
            to = lax.broadcasted_iota(jnp.int32, (high, wide), 1) + side
            part = jnp.where(at == to, 1.0, 0.0) - exact_dot(z[i, rows, :], full[:, cols])
            rest[rows, cols] = part
            return total + jnp.sum(part * part)

        tiles = w // high * across
        total = lax.fori_loop(0, tiles, residual, jnp.float32(0.0))
        spread[...] = emb(z[i])

        def correct(k, _):
            _, _, rows, cols = cut(k)
            z[i, rows, cols] += exact_dot(rest[rows, :], spread[:, cols])
            return 0

        lax.fori_loop(0, tiles, correct, 0)
        return state[0] + 1, total

    lax.while_loop(
        lambda state: (state[0] < 64) & jnp.logical_not(state[1] <= 1e-6),
        once,
        (0, jnp.float32(1.0)),
    )


def initial(onsite, scalars):
    w = onsite.shape[0]
    at = lax.broadcasted_iota(jnp.int32, (w, 2 * w), 0)
    to = lax.broadcasted_iota(jnp.int32, (w, 2 * w), 1)
    shift = jnp.where(at == to, scalars[0], jnp.where(at + w == to, scalars[1], 0.0))
    return shift - onsite


def deferred(out, k, a, b, sign):
    a_high, a_low = split(a)
    b_high, b_low = split(b)

    def lead():
        put(out.at[k], sign * dot(a_high, emb(b_high)))

    def middle():
        put(out.at[k], row(out[k]) + sign * dot(a_high, emb(b_low)))

    def trail():
        put(out.at[k], row(out[k]) + sign * dot(a_low, emb(b_high)))

    return lead, middle, trail


def paired(first, second):
    def piece():
        first()
        second()

    return piece


def solve(d, couplings, side, eta, payload, work):
    invert([d], eta, work, side)
    z = split(work[0][0])
    for k in range(2):
        put(payload, times(z, row(couplings[1 - k])), k * d.shape[1])


def part(payload, k):
    rows = 2 * payload.shape[1]
    return row(payload[pl.ds(pl.multiple_of(k * rows, rows), rows)])


def sides(parity):
    return 1 - parity, parity


def first_kernel(onsite, hop, scalars, up, down, sem, *work):
    w = onsite.shape[2]
    beside = pltpu.make_async_copy(hop.at[0], down.at[pl.ds(2 * w, 2 * w)], sem)
    beside.start()
    invert([initial(row(onsite[i]), scalars) for i in range(2)], scalars[1], work)
    put(up, work[0][1])
    put(down, work[0][0])
    beside.wait()


def near_kernel(
    onsite, hop, hop_left, z_b, z_hop_a, scalars, d_a, d_b, u_a, l_b, g_a, k_a, *outputs
):
    h = row(hop[0])
    before = row(hop_left[1])
    put(g_a, adjoint(before))
    put(k_a, adjoint(row(hop_left[0])))
    t = product(h, row(z_b[...]))
    put(d_a, initial(row(onsite[0]), scalars) - product(t, adjoint(h)))
    put(u_a, product(t, row(hop[1])) * (-scalars[2]))
    t = product(adjoint(h), part(z_hop_a, 0))
    put(d_b, initial(row(onsite[1]), scalars) - product(t, h))
    put(l_b, -product(t, adjoint(before)))


def second_kernel(d_in, c_in, g, z, k, scalars, side, d_out, c_out, payload, *work):
    at = side[0]
    gain = row(g[...])
    t = product(gain, row(z[...]))
    put(d_out, row(d_in[...]) - product(t, adjoint(gain)))
    c_out[1 - at] = c_in[...]
    pieces = deferred(c_out, at, t, row(k[...]), -1.0)
    solve(row(d_out[...]), c_out, pieces, scalars[1], payload, work)


def third_kernel(d_in, c_in, even, odd, scalars, parity, d_out, c_out, payload, *work):
    i, j = sides(parity[0])
    one, two = row(c_in[i]), row(c_in[j])
    d = row(d_in[...]) - product(one, part(even, i)) - product(two, part(odd, j))
    put(d_out, d)
    set_one = deferred(c_out, i, one, part(even, 1 - i), -1.0)
    set_two = deferred(c_out, j, two, part(odd, 1 - j), -1.0)
    side = [paired(*pair) for pair in zip(set_one, set_two)]
    solve(row(d_out[...]), c_out, side, scalars[1], payload, work)


def last_kernel(k, d_in, c_in, even, odd, ints, c_old, *refs):
    d_out, c_out = refs[-4:-2]
    hold, sems = refs[-2:]
    slab = ints[2]
    is_even = sides(ints[1])[0] == k
    to_d = row(jnp.where(is_even, even[...], odd[...]))
    to_c = row(jnp.where(is_even, odd[...], even[...]))
    put(hold.at[0], -product(row(c_in[1 - k]), to_c))
    copies = [pltpu.make_async_copy(hold.at[0], c_out.at[slab], sems.at[0])]
    copies[0].start()
    d = row(d_in[...]) - product(row(c_in[k]), to_d)
    if k == 0:
        put(d_out, d)
    else:
        put(hold.at[1], d)
        copies.append(pltpu.make_async_copy(hold.at[1], d_out.at[slab], sems.at[1]))
        copies[1].start()
    for copy in copies:
        copy.wait()


def shape(*dims):
    return jax.ShapeDtypeStruct(dims, F32)


def work(count, w):
    return [
        pltpu.VMEM((count, w, 2 * w), F32),
        pltpu.VMEM((count, 2 * w, 2 * w), BF),
        pltpu.VMEM((count, 2 * w, 2 * w), BF),
        pltpu.VMEM((count, 2 * w, 2 * w), BF),
        pltpu.VMEM((2 * w, 2 * w), F32),
        pltpu.VMEM((2 * w, 2 * w), F32),
        pltpu.VMEM((w, 2 * w), F32),
    ]


PARAMS = pltpu.CompilerParams(vmem_limit_bytes=20 << 20)


def send(x, by):
    size = lax.axis_size("slab")
    return lax.ppermute(x, "slab", [(i, i + by) for i in range(size) if 0 <= i + by < size])


def swaps(x, by):
    size = lax.axis_size("slab")
    even, odd = [], []
    for i in range(size - by):
        pairs = odd if i // by % 2 else even
        pairs += [(i, i + by), (i + by, i)]
    from_odd = lax.ppermute(x, "slab", odd)
    from_even = lax.ppermute(x, "slab", even)
    return from_even, from_odd


def reduce_levels(onsite, hop, energy_level, broadening):
    rows, _, w, _ = onsite.shape
    onsite = onsite.reshape(rows, 2 * w, w)
    hop = hop.reshape(rows, 2 * w, w)
    last = lax.axis_index("slab") == lax.axis_size("slab") - 1
    keep = jnp.where(last, 0.0, 1.0).astype(F32)
    scalars = jnp.stack([energy_level[0], broadening[0], keep])
    position = lax.axis_index("slab")
    near, far = position & 1, (position >> 1) & 1
    at_a, at_b = (jnp.stack([near, far, jnp.int32(k)]) for k in range(2))
    scalars, at_a, at_b = lax.optimization_barrier((scalars, at_a, at_b))

    hop_left = send(hop, 1)
    block, pair, two = shape(2 * w, w), shape(4 * w, w), shape(2, 2 * w, w)
    up, down = pl.pallas_call(
        first_kernel,
        out_shape=(block, pair),
        in_specs=[VMEM, pl.BlockSpec(memory_space=pl.ANY), SMEM],
        out_specs=(VMEM,) * 2,
        scratch_shapes=[pltpu.SemaphoreType.DMA] + work(rows, w),
        compiler_params=PARAMS,
        name="first",
    )(onsite, pltpu.with_memory_space_constraint(hop, pltpu.HBM), scalars)
    z_left = send(up, 1)
    z_hop_right = send(down, -1)
    whole = shape(rows, 2 * w, w)
    kept = pl.BlockSpec(memory_space=pl.ANY)
    d_a, d_b, u_a, l_b, g_a, k_a, d_out, u_out, l_out = pl.pallas_call(
        near_kernel,
        out_shape=(block,) * 6 + (whole,) * 3,
        in_specs=[VMEM] * 5 + [SMEM],
        out_specs=(VMEM,) * 6 + (kept,) * 3,
        compiler_params=PARAMS,
        name="near",
    )(onsite, hop, hop_left, up, down, scalars)

    second = pl.pallas_call(
        second_kernel,
        out_shape=(block, two, pair),
        in_specs=[VMEM] * 5 + [SMEM] * 2,
        out_specs=(VMEM,) * 3,
        scratch_shapes=work(1, w),
        compiler_params=PARAMS,
        name="second",
    )
    d_a, c_a, p_a = second(d_a, u_a, g_a, z_left, k_a, scalars, jnp.zeros((1,), jnp.int32))
    even_a, odd_a = swaps(p_a, 1)
    d_b, c_b, p_b = second(
        d_b,
        l_b,
        hop[1],
        z_hop_right[: 2 * w],
        z_hop_right[2 * w :],
        scalars,
        jnp.ones((1,), jnp.int32),
    )
    even_b, odd_b = swaps(p_b, 1)

    third = pl.pallas_call(
        third_kernel,
        out_shape=(block, two, pair),
        in_specs=[VMEM] * 4 + [SMEM] * 2,
        out_specs=(VMEM,) * 3,
        scratch_shapes=work(1, w),
        compiler_params=PARAMS,
        name="third",
    )
    d_a, c_a, p_a = third(d_a, c_a, even_a, odd_a, scalars, at_a)
    even_a, odd_a = swaps(p_a, 2)
    d_b, c_b, p_b = third(d_b, c_b, even_b, odd_b, scalars, at_a)
    first_b = swaps(p_b[: 2 * w], 2)
    second_b = swaps(p_b[2 * w :], 2)

    hold = [pltpu.VMEM((2, 2 * w, w), F32), pltpu.SemaphoreType.DMA((2,))]
    take_upper = pl.pallas_call(
        functools.partial(last_kernel, 0),
        out_shape=(block, whole),
        in_specs=[VMEM] * 4 + [SMEM, kept],
        out_specs=(VMEM, kept),
        input_output_aliases={5: 1},
        scratch_shapes=hold,
        compiler_params=PARAMS,
        name="take_upper",
    )
    take_lower = pl.pallas_call(
        functools.partial(last_kernel, 1),
        out_shape=(whole, whole),
        in_specs=[VMEM] * 4 + [SMEM, kept, kept],
        out_specs=(kept, kept),
        input_output_aliases={5: 1, 6: 0},
        scratch_shapes=hold,
        compiler_params=PARAMS,
        name="take_lower",
    )
    d_a, u_out = take_upper(d_a, c_a, even_a[: 2 * w], odd_a[: 2 * w], at_a, u_out)
    d_out, l_out = take_lower(
        d_a, c_a, even_a[2 * w :], odd_a[2 * w :], at_a, l_out, d_out
    )
    d_b, u_out = take_upper(d_b, c_b, *first_b, at_b, u_out)
    d_out, l_out = take_lower(d_b, c_b, *second_b, at_b, l_out, d_out)
    return tuple(x.reshape(rows, 2, w, w) for x in (d_out, u_out, l_out))


def solution(mesh):
    placed = (P("slab", None, None, None), P("slab", None, None, None), P("energy"), P("energy"))
    out = P(("energy", "slab"), None, None, None)
    return jax.shard_map(
        reduce_levels, mesh=mesh, in_specs=placed, out_specs=(out, out, out), check_vma=False
    )
```

```python
import functools

import jax
import jax.numpy as jnp
from jax import lax
from jax.experimental import pallas as pl
from jax.experimental.pallas import tpu as pltpu
from jax.sharding import PartitionSpec as P


BF = jnp.bfloat16
F32 = jnp.float32
HIGHEST = lax.Precision.HIGHEST
CONVERGED = 0.985
TRUSTED = 0.012
VMEM = pl.BlockSpec(memory_space=pltpu.VMEM)
SMEM = pl.BlockSpec(memory_space=pltpu.SMEM)


def dot(a, b):
    return jnp.dot(a, b, preferred_element_type=F32)


def exact_dot(a, b):
    return jnp.dot(a, b, precision=HIGHEST, preferred_element_type=F32)


def row(c):
    h = c.shape[0] // 2
    return jnp.concatenate([c[:h], c[h:]], axis=1)


def put(out, r, at=0):
    h, w = r.shape[0], r.shape[1] // 2
    out[at : at + h] = r[:, :w]
    out[at + h : at + 2 * h] = r[:, w:]


def turned(r):
    w = r.shape[1] // 2
    return jnp.concatenate([-r[:, w:], r[:, :w]], axis=1)


def emb(r):
    return jnp.concatenate([r, turned(r)], axis=0)


def adjoint(r):
    w = r.shape[0]
    return jnp.concatenate([r[:, :w].T, -r[:, w:].T], axis=1)


def split(x):
    high = x.astype(BF)
    return high, (x - high.astype(F32)).astype(BF)


def product(a, b):
    return times(split(a), b)


def times(a, b):
    return multiply(a, split(b))


def multiply(a, b):
    a_high, a_low = a
    b_high, b_low = b
    e_high, e_low = emb(b_high), emb(b_low)
    return dot(a_high, e_high) + dot(a_high, e_low) + dot(a_low, e_high)


def unit(w):
    at = lax.broadcasted_iota(jnp.int32, (w, 2 * w), 0)
    return (at == lax.broadcasted_iota(jnp.int32, (w, 2 * w), 1)).astype(F32)


def invert(blocks, eta, work, side=()):
    z, ea, el, ex, full, spread, rest = work
    w = blocks[0].shape[0]
    one = unit(w)
    halves = [slice(k * w // 2, (k + 1) * w // 2) for k in range(2)]

    def place(i, x):
        ex[i, :w] = x
        ex[i, w:] = turned(x)

    norms, grams = [], []
    for i, a in enumerate(blocks):
        high, low = split(a)
        ea[i] = emb(high)
        el[i] = emb(low)
        ah = adjoint(high)
        gram = dot(ah, ea[i])
        size = jnp.sqrt(gram[:, :w] * gram[:, :w] + gram[:, w:] * gram[:, w:])
        norm = 1.02 * jnp.max(jnp.sum(size, axis=1))
        place(i, (ah.astype(F32) * (1.0 / norm)).astype(BF))
        norms.append(norm)
        grams.append(gram)
    largest = functools.reduce(jnp.maximum, norms)
    bound = jnp.maximum(0.9 * eta * eta / largest, 1e-10)

    def step(bound, piece=None, known=None):
        mu = 2.0 / (bound + 1.03)
        for i in range(len(blocks)):
            if known is None:
                errors = [(one[h] - mu * dot(ex[i, h], ea[i])).astype(BF) for h in halves]
            else:
                errors = [(one[h] - (mu / norms[i]) * known[i][h]).astype(BF) for h in halves]
            if piece is not None:
                piece()
            news = [
                (mu * (ex[i, h].astype(F32) + dot(e, ex[i]))).astype(BF)
                for h, e in zip(halves, errors)
            ]
            place(i, jnp.concatenate(news, axis=0))
        gap = 1.0 - mu * bound
        return 1.0 - gap * gap

    bound = step(bound, side[0] if side else None, grams)
    for piece in side[1:]:
        bound = step(bound, piece)
    lax.while_loop(lambda bound: bound < CONVERGED, step, bound)
    for i, a in enumerate(blocks):
        x = ex[i, :w]
        error = one - (dot(x, ea[i]) + dot(x, el[i]))
        z[i] = x.astype(F32) + dot(error.astype(BF), ex[i])
        left = jnp.sum(error * error)

        @pl.when(jnp.logical_not(left <= TRUSTED))
        def _():
            polish(a, norms[i], left, z, i, full, spread, rest)


def polish(a, norm, left, z, i, full, spread, rest):
    w = a.shape[0]
    high, wide = min(32, w), min(128, w)
    across = 2 * w // wide
    full[...] = emb(a)

    @pl.when(jnp.logical_not(left <= 0.25))
    def _():
        z[i] = adjoint(a) * (1.0 / norm)

    def cut(k):
        top, side = k // across * high, k % across * wide
        return (
            top,
            side,
            pl.ds(pl.multiple_of(top, high), high),
            pl.ds(pl.multiple_of(side, wide), wide),
        )

    def once(state):
        def residual(k, total):
            top, side, rows, cols = cut(k)
            at = lax.broadcasted_iota(jnp.int32, (high, wide), 0) + top
            to = lax.broadcasted_iota(jnp.int32, (high, wide), 1) + side
            part = jnp.where(at == to, 1.0, 0.0) - exact_dot(z[i, rows, :], full[:, cols])
            rest[rows, cols] = part
            return total + jnp.sum(part * part)

        tiles = w // high * across
        total = lax.fori_loop(0, tiles, residual, jnp.float32(0.0))
        spread[...] = emb(z[i])

        def correct(k, _):
            _, _, rows, cols = cut(k)
            z[i, rows, cols] += exact_dot(rest[rows, :], spread[:, cols])
            return 0

        lax.fori_loop(0, tiles, correct, 0)
        return state[0] + 1, total

    lax.while_loop(
        lambda state: (state[0] < 64) & jnp.logical_not(state[1] <= 1e-6),
        once,
        (0, jnp.float32(1.0)),
    )


def initial(onsite, scalars):
    w = onsite.shape[0]
    at = lax.broadcasted_iota(jnp.int32, (w, 2 * w), 0)
    to = lax.broadcasted_iota(jnp.int32, (w, 2 * w), 1)
    shift = jnp.where(at == to, scalars[0], jnp.where(at + w == to, scalars[1], 0.0))
    return shift - onsite


def deferred(out, k, a, b, sign):
    a_high, a_low = split(a)
    b_high, b_low = split(b)

    def lead():
        put(out.at[k], sign * dot(a_high, emb(b_high)))

    def middle():
        put(out.at[k], row(out[k]) + sign * dot(a_high, emb(b_low)))

    def trail():
        put(out.at[k], row(out[k]) + sign * dot(a_low, emb(b_high)))

    return lead, middle, trail


def paired(first, second):
    def piece():
        first()
        second()

    return piece


def solve(d, couplings, side, eta, payload, work):
    invert([d], eta, work, side)
    z = split(work[0][0])
    for k in range(2):
        put(payload, times(z, row(couplings[1 - k])), k * d.shape[1])


def part(payload, k):
    rows = 2 * payload.shape[1]
    return row(payload[pl.ds(pl.multiple_of(k * rows, rows), rows)])


def sides(parity):
    return 1 - parity, parity


def first_kernel(onsite, hop, scalars, up, down, sem, *work):
    w = onsite.shape[2]
    beside = pltpu.make_async_copy(hop.at[0], down.at[pl.ds(2 * w, 2 * w)], sem)
    beside.start()
    invert([initial(row(onsite[i]), scalars) for i in range(2)], scalars[1], work)
    put(up, work[0][1])
    put(down, work[0][0])
    beside.wait()


def near_kernel(
    onsite, hop, hop_left, z_b, z_hop_a, scalars, d_a, d_b, u_a, l_b, g_a, g_b, k_a, *outputs
):
    h = row(hop[0])
    h_adj = adjoint(h)
    before, after = row(hop_left[1]), row(hop[1])
    before_adj = adjoint(before)
    for out, pair in ((g_a, (before_adj, before)), (g_b, (after, adjoint(after)))):
        for k, value in enumerate(pair):
            out[2 * k], out[2 * k + 1] = split(value)
    put(k_a, adjoint(row(hop_left[0])))
    t = product(h, row(z_b[...]))
    put(d_a, initial(row(onsite[0]), scalars) - product(t, h_adj))
    put(u_a, product(t, after) * (-scalars[2]))
    t = product(h_adj, part(z_hop_a, 0))
    put(d_b, initial(row(onsite[1]), scalars) - product(t, h))
    put(l_b, -product(t, before_adj))


def second_kernel(d_in, c_in, g, z, k, scalars, side, d_out, c_out, payload, *work):
    at = side[0]
    t = times((g[0], g[1]), row(z[...]))
    put(d_out, row(d_in[...]) - multiply(split(t), (g[2], g[3])))
    c_out[1 - at] = c_in[...]
    pieces = deferred(c_out, at, t, row(k[...]), -1.0)
    solve(row(d_out[...]), c_out, pieces, scalars[1], payload, work)


def third_kernel(d_in, c_in, even, odd, scalars, parity, d_out, c_out, payload, *work):
    i, j = sides(parity[0])
    one, two = row(c_in[i]), row(c_in[j])
    d = row(d_in[...]) - product(one, part(even, i)) - product(two, part(odd, j))
    put(d_out, d)
    set_one = deferred(c_out, i, one, part(even, 1 - i), -1.0)
    set_two = deferred(c_out, j, two, part(odd, 1 - j), -1.0)
    side = [paired(*pair) for pair in zip(set_one, set_two)]
    solve(row(d_out[...]), c_out, side, scalars[1], payload, work)


def last_kernel(k, start, d_in, c_in, even, odd, ints, c_old, *refs):
    d_out, c_out = refs[-4:-2]
    hold, sems = refs[-2:]
    slab = ints[2]
    wide = even.shape[1]
    cols = pl.ds(start, wide)
    is_even = sides(ints[1])[0] == k
    to_d = row(jnp.where(is_even, even[...], odd[...]))
    to_c = row(jnp.where(is_even, odd[...], even[...]))
    put(hold.at[0], -product(row(c_in[1 - k]), to_c))
    copies = [pltpu.make_async_copy(hold.at[0], c_out.at[slab, :, cols], sems.at[0])]
    copies[0].start()
    d = row(d_in[:, start : start + wide]) - product(row(c_in[k]), to_d)
    if k == 0:
        put(d_out, d)
    else:
        put(hold.at[1], d)
        copies.append(pltpu.make_async_copy(hold.at[1], d_out.at[slab, :, cols], sems.at[1]))
        copies[1].start()
    for copy in copies:
        copy.wait()


def shape(*dims):
    return jax.ShapeDtypeStruct(dims, F32)


def work(count, w):
    return [
        pltpu.VMEM((count, w, 2 * w), F32),
        pltpu.VMEM((count, 2 * w, 2 * w), BF),
        pltpu.VMEM((count, 2 * w, 2 * w), BF),
        pltpu.VMEM((count, 2 * w, 2 * w), BF),
        pltpu.VMEM((2 * w, 2 * w), F32),
        pltpu.VMEM((2 * w, 2 * w), F32),
        pltpu.VMEM((w, 2 * w), F32),
    ]


PARAMS = pltpu.CompilerParams(vmem_limit_bytes=20 << 20)


def send(x, by):
    size = lax.axis_size("slab")
    return lax.ppermute(x, "slab", [(i, i + by) for i in range(size) if 0 <= i + by < size])


def swaps(x, by):
    size = lax.axis_size("slab")
    even, odd = [], []
    for i in range(size - by):
        pairs = odd if i // by % 2 else even
        pairs += [(i, i + by), (i + by, i)]
    from_odd = lax.ppermute(x, "slab", odd)
    from_even = lax.ppermute(x, "slab", even)
    return from_even, from_odd


def reduce_levels(onsite, hop, energy_level, broadening):
    rows, _, w, _ = onsite.shape
    onsite = onsite.reshape(rows, 2 * w, w)
    hop = hop.reshape(rows, 2 * w, w)
    last = lax.axis_index("slab") == lax.axis_size("slab") - 1
    keep = jnp.where(last, 0.0, 1.0).astype(F32)
    scalars = jnp.stack([energy_level[0], broadening[0], keep])
    position = lax.axis_index("slab")
    near, far = position & 1, (position >> 1) & 1
    at_a, at_b = (jnp.stack([near, far, jnp.int32(k)]) for k in range(2))
    scalars, at_a, at_b = lax.optimization_barrier((scalars, at_a, at_b))

    hop_left = send(hop, 1)
    block, pair, two = shape(2 * w, w), shape(4 * w, w), shape(2, 2 * w, w)
    up, down = pl.pallas_call(
        first_kernel,
        out_shape=(block, pair),
        in_specs=[VMEM, pl.BlockSpec(memory_space=pl.ANY), SMEM],
        out_specs=(VMEM,) * 2,
        scratch_shapes=[pltpu.SemaphoreType.DMA] + work(rows, w),
        compiler_params=PARAMS,
        name="first",
    )(onsite, pltpu.with_memory_space_constraint(hop, pltpu.HBM), scalars)
    z_left = send(up, 1)
    z_hop_right = send(down, -1)
    whole = shape(rows, 2 * w, w)
    kept = pl.BlockSpec(memory_space=pl.ANY)
    gain = jax.ShapeDtypeStruct((4, w, 2 * w), BF)
    d_a, d_b, u_a, l_b, g_a, g_b, k_a, d_out, u_out, l_out = pl.pallas_call(
        near_kernel,
        out_shape=(block,) * 4 + (gain, gain, block) + (whole,) * 3,
        in_specs=[VMEM] * 5 + [SMEM],
        out_specs=(VMEM,) * 7 + (kept,) * 3,
        compiler_params=PARAMS,
        name="near",
    )(onsite, hop, hop_left, up, down, scalars)

    second = pl.pallas_call(
        second_kernel,
        out_shape=(block, two, pair),
        in_specs=[VMEM] * 5 + [SMEM] * 2,
        out_specs=(VMEM,) * 3,
        scratch_shapes=work(1, w),
        compiler_params=PARAMS,
        name="second",
    )
    d_a, c_a, p_a = second(d_a, u_a, g_a, z_left, k_a, scalars, jnp.zeros((1,), jnp.int32))
    even_a, odd_a = swaps(p_a, 1)
    d_b, c_b, p_b = second(
        d_b,
        l_b,
        g_b,
        z_hop_right[: 2 * w],
        z_hop_right[2 * w :],
        scalars,
        jnp.ones((1,), jnp.int32),
    )
    even_b, odd_b = swaps(p_b, 1)

    third = pl.pallas_call(
        third_kernel,
        out_shape=(block, two, pair),
        in_specs=[VMEM] * 4 + [SMEM] * 2,
        out_specs=(VMEM,) * 3,
        scratch_shapes=work(1, w),
        compiler_params=PARAMS,
        name="third",
    )
    d_a, c_a, p_a = third(d_a, c_a, even_a, odd_a, scalars, at_a)
    even_a, odd_a = swaps(p_a, 2)
    d_b, c_b, p_b = third(d_b, c_b, even_b, odd_b, scalars, at_a)
    first_b = swaps(p_b[: 2 * w], 2)
    cuts = (0, w // 2)
    lower_b = [swaps(p_b[2 * w :, cut : cut + w // 2], 2) for cut in cuts]

    def hold(wide):
        return [pltpu.VMEM((2, 2 * w, wide), F32), pltpu.SemaphoreType.DMA((2,))]

    take_upper = pl.pallas_call(
        functools.partial(last_kernel, 0, 0),
        out_shape=(block, whole),
        in_specs=[VMEM] * 4 + [SMEM, kept],
        out_specs=(VMEM, kept),
        input_output_aliases={5: 1},
        scratch_shapes=hold(w),
        compiler_params=PARAMS,
        name="take_upper",
    )
    take_lower = [
        pl.pallas_call(
            functools.partial(last_kernel, 1, cut),
            out_shape=(whole, whole),
            in_specs=[VMEM] * 4 + [SMEM, kept, kept],
            out_specs=(kept, kept),
            input_output_aliases={5: 1, 6: 0},
            scratch_shapes=hold(w // 2),
            compiler_params=PARAMS,
        )
        for cut in cuts
    ]
    d_a, u_out = take_upper(d_a, c_a, even_a[: 2 * w], odd_a[: 2 * w], at_a, u_out)
    for take, cut in zip(take_lower, cuts):
        arrived = (x[2 * w :, cut : cut + w // 2] for x in (even_a, odd_a))
        d_out, l_out = take(d_a, c_a, *arrived, at_a, l_out, d_out)
    d_b, u_out = take_upper(d_b, c_b, *first_b, at_b, u_out)
    for take, arrived in zip(take_lower, lower_b):
        d_out, l_out = take(d_b, c_b, *arrived, at_b, l_out, d_out)
    return tuple(x.reshape(rows, 2, w, w) for x in (d_out, u_out, l_out))


def solution(mesh):
    placed = (P("slab", None, None, None), P("slab", None, None, None), P("energy"), P("energy"))
    out = P(("energy", "slab"), None, None, None)
    return jax.shard_map(
        reduce_levels, mesh=mesh, in_specs=placed, out_specs=(out, out, out), check_vma=False
    )
```

```python
import functools

import jax
import jax.numpy as jnp
from jax import lax
from jax.experimental import pallas as pl
from jax.experimental.pallas import tpu as pltpu
from jax.sharding import PartitionSpec as P


BF = jnp.bfloat16
F32 = jnp.float32
HIGHEST = lax.Precision.HIGHEST
CONVERGED = 0.985
TRUSTED = 0.012
VMEM = pl.BlockSpec(memory_space=pltpu.VMEM)
SMEM = pl.BlockSpec(memory_space=pltpu.SMEM)


def dot(a, b):
    return jnp.dot(a, b, preferred_element_type=F32)


def exact_dot(a, b):
    return jnp.dot(a, b, precision=HIGHEST, preferred_element_type=F32)


def row(c):
    h = c.shape[0] // 2
    return jnp.concatenate([c[:h], c[h:]], axis=1)


def put(out, r, at=0):
    h, w = r.shape[0], r.shape[1] // 2
    out[at : at + h] = r[:, :w]
    out[at + h : at + 2 * h] = r[:, w:]


def turned(r):
    w = r.shape[1] // 2
    return jnp.concatenate([-r[:, w:], r[:, :w]], axis=1)


def emb(r):
    return jnp.concatenate([r, turned(r)], axis=0)


def adjoint(r):
    w = r.shape[0]
    return jnp.concatenate([r[:, :w].T, -r[:, w:].T], axis=1)


def split(x):
    high = x.astype(BF)
    return high, (x - high.astype(F32)).astype(BF)


def product(a, b):
    return times(split(a), b)


def times(a, b):
    return multiply(a, split(b))


def multiply(a, b):
    a_high, a_low = a
    b_high, b_low = b
    e_high, e_low = emb(b_high), emb(b_low)
    return dot(a_high, e_high) + dot(a_high, e_low) + dot(a_low, e_high)


def unit(w):
    at = lax.broadcasted_iota(jnp.int32, (w, 2 * w), 0)
    return (at == lax.broadcasted_iota(jnp.int32, (w, 2 * w), 1)).astype(F32)


def invert(blocks, eta, work, side=()):
    z, ea, el, ex, full, spread, rest = work
    w = blocks[0].shape[0]
    one = unit(w)
    halves = [slice(k * w // 2, (k + 1) * w // 2) for k in range(2)]

    def place(i, x):
        ex[i, :w] = x
        ex[i, w:] = turned(x)

    norms, grams = [], []
    for i, a in enumerate(blocks):
        high, low = split(a)
        ea[i] = emb(high)
        el[i] = emb(low)
        ah = adjoint(high)
        gram = dot(ah, ea[i])
        size = jnp.sqrt(gram[:, :w] * gram[:, :w] + gram[:, w:] * gram[:, w:])
        norm = 1.02 * jnp.max(jnp.sum(size, axis=1))
        place(i, (ah.astype(F32) * (1.0 / norm)).astype(BF))
        norms.append(norm)
        grams.append(gram)
    largest = functools.reduce(jnp.maximum, norms)
    bound = jnp.maximum(0.9 * eta * eta / largest, 1e-10)

    def step(bound, piece=None, known=None):
        mu = 2.0 / (bound + 1.03)
        for i in range(len(blocks)):
            if known is None:
                errors = [(one[h] - mu * dot(ex[i, h], ea[i])).astype(BF) for h in halves]
            else:
                errors = [(one[h] - (mu / norms[i]) * known[i][h]).astype(BF) for h in halves]
            if piece is not None:
                piece()
            news = [
                (mu * (ex[i, h].astype(F32) + dot(e, ex[i]))).astype(BF)
                for h, e in zip(halves, errors)
            ]
            place(i, jnp.concatenate(news, axis=0))
        gap = 1.0 - mu * bound
        return 1.0 - gap * gap

    bound = step(bound, side[0] if side else None, grams)
    for piece in side[1:]:
        bound = step(bound, piece)
    lax.while_loop(lambda bound: bound < CONVERGED, step, bound)
    for i, a in enumerate(blocks):
        x = ex[i, :w]
        error = one - (dot(x, ea[i]) + dot(x, el[i]))
        z[i] = x.astype(F32) + dot(error.astype(BF), ex[i])
        left = jnp.sum(error * error)

        @pl.when(jnp.logical_not(left <= TRUSTED))
        def _():
            polish(a, norms[i], left, z, i, full, spread, rest)


def polish(a, norm, left, z, i, full, spread, rest):
    w = a.shape[0]
    high, wide = min(32, w), min(128, w)
    across = 2 * w // wide
    full[...] = emb(a)

    @pl.when(jnp.logical_not(left <= 0.25))
    def _():
        z[i] = adjoint(a) * (1.0 / norm)

    def cut(k):
        top, side = k // across * high, k % across * wide
        return (
            top,
            side,
            pl.ds(pl.multiple_of(top, high), high),
            pl.ds(pl.multiple_of(side, wide), wide),
        )

    def once(state):
        def residual(k, total):
            top, side, rows, cols = cut(k)
            at = lax.broadcasted_iota(jnp.int32, (high, wide), 0) + top
            to = lax.broadcasted_iota(jnp.int32, (high, wide), 1) + side
            part = jnp.where(at == to, 1.0, 0.0) - exact_dot(z[i, rows, :], full[:, cols])
            rest[rows, cols] = part
            return total + jnp.sum(part * part)

        tiles = w // high * across
        total = lax.fori_loop(0, tiles, residual, jnp.float32(0.0))
        spread[...] = emb(z[i])

        def correct(k, _):
            _, _, rows, cols = cut(k)
            z[i, rows, cols] += exact_dot(rest[rows, :], spread[:, cols])
            return 0

        lax.fori_loop(0, tiles, correct, 0)
        return state[0] + 1, total

    lax.while_loop(
        lambda state: (state[0] < 64) & jnp.logical_not(state[1] <= 1e-6),
        once,
        (0, jnp.float32(1.0)),
    )


def initial(onsite, scalars):
    w = onsite.shape[0]
    at = lax.broadcasted_iota(jnp.int32, (w, 2 * w), 0)
    to = lax.broadcasted_iota(jnp.int32, (w, 2 * w), 1)
    shift = jnp.where(at == to, scalars[0], jnp.where(at + w == to, scalars[1], 0.0))
    return shift - onsite


def deferred(out, k, a, b, sign):
    a_high, a_low = split(a)
    b_high, b_low = split(b)

    def lead():
        put(out.at[k], sign * dot(a_high, emb(b_high)))

    def middle():
        put(out.at[k], row(out[k]) + sign * dot(a_high, emb(b_low)))

    def trail():
        put(out.at[k], row(out[k]) + sign * dot(a_low, emb(b_high)))

    return lead, middle, trail


def paired(first, second):
    def piece():
        first()
        second()

    return piece


def solve(d, couplings, side, eta, payload, work):
    invert([d], eta, work, side)
    z = split(work[0][0])
    for k in range(2):
        put(payload, times(z, row(couplings[1 - k])), k * d.shape[1])


def part(payload, k):
    rows = 2 * payload.shape[1]
    return row(payload[pl.ds(pl.multiple_of(k * rows, rows), rows)])


def sides(parity):
    return 1 - parity, parity


def first_kernel(onsite, scalars, ints, z_even, z_odd, z_own, *work):
    invert([initial(row(onsite[i]), scalars) for i in range(2)], scalars[1], work)
    for i in range(2):
        put(z_own.at[i], work[0][i])
    put(z_even, work[0][1 - ints[0]])
    put(z_odd, work[0][ints[0]])


def near_kernel(
    onsite, hop, hop_even, hop_odd, z, scalars, ints, d_out, c_out, g_out, k_out, *outputs
):
    run_b = ints[0]
    run_a = 1 - run_b
    left = [jnp.where(run_b == 0, hop_odd[k], hop_even[k]) for k in range(2)]
    right = jnp.where(run_b == 0, hop_even[0], hop_odd[0])
    h = row(hop[0])
    h_adj = adjoint(h)
    before, after = row(left[1]), row(hop[1])
    before_adj = adjoint(before)
    for run, pair in ((run_a, (before_adj, before)), (run_b, (after, adjoint(after)))):
        for k, value in enumerate(pair):
            high, low = split(value)
            g_out[run, 2 * k] = high
            g_out[run, 2 * k + 1] = low
    put(k_out.at[run_a], adjoint(row(left[0])))
    k_out[run_b] = right
    t = product(h, row(z[1]))
    put(d_out.at[run_a], initial(row(onsite[0]), scalars) - product(t, h_adj))
    put(c_out.at[run_a], product(t, after) * (-scalars[2]))
    t = product(h_adj, row(z[0]))
    put(d_out.at[run_b], initial(row(onsite[1]), scalars) - product(t, h))
    put(c_out.at[run_b], -product(t, before_adj))


def second_kernel(d_in, c_in, g, z, k, scalars, ints, d_out, c_out, payload, *work):
    run, at = ints[0], ints[1]
    t = times((g[run, 0], g[run, 1]), row(z[...]))
    put(d_out, row(d_in[run]) - multiply(split(t), (g[run, 2], g[run, 3])))
    c_out[1 - at] = c_in[run]
    pieces = deferred(c_out, at, t, row(k[run]), -1.0)
    solve(row(d_out[...]), c_out, pieces, scalars[1], payload, work)


def third_kernel(d_in, c_in, even, odd, scalars, parity, d_out, c_out, payload, *work):
    i, j = sides(parity[0])
    one, two = row(c_in[i]), row(c_in[j])
    d = row(d_in[...]) - product(one, part(even, i)) - product(two, part(odd, j))
    put(d_out, d)
    set_one = deferred(c_out, i, one, part(even, 1 - i), -1.0)
    set_two = deferred(c_out, j, two, part(odd, 1 - j), -1.0)
    side = [paired(*pair) for pair in zip(set_one, set_two)]
    solve(row(d_out[...]), c_out, side, scalars[1], payload, work)


def last_kernel(k, start, d_in, c_in, even, odd, ints, c_old, *refs):
    d_out, c_out = refs[-4:-2]
    hold, sems = refs[-2:]
    slab = ints[2]
    wide = even.shape[1]
    cols = pl.ds(start, wide)
    is_even = sides(ints[1])[0] == k
    to_d = row(jnp.where(is_even, even[...], odd[...]))
    to_c = row(jnp.where(is_even, odd[...], even[...]))
    put(hold.at[0], -product(row(c_in[1 - k]), to_c))
    copies = [pltpu.make_async_copy(hold.at[0], c_out.at[slab, :, cols], sems.at[0])]
    copies[0].start()
    d = row(d_in[:, start : start + wide]) - product(row(c_in[k]), to_d)
    if k == 0:
        put(d_out, d)
    else:
        put(hold.at[1], d)
        copies.append(pltpu.make_async_copy(hold.at[1], d_out.at[slab, :, cols], sems.at[1]))
        copies[1].start()
    for copy in copies:
        copy.wait()


def shape(*dims):
    return jax.ShapeDtypeStruct(dims, F32)


def work(count, w):
    return [
        pltpu.VMEM((count, w, 2 * w), F32),
        pltpu.VMEM((count, 2 * w, 2 * w), BF),
        pltpu.VMEM((count, 2 * w, 2 * w), BF),
        pltpu.VMEM((count, 2 * w, 2 * w), BF),
        pltpu.VMEM((2 * w, 2 * w), F32),
        pltpu.VMEM((2 * w, 2 * w), F32),
        pltpu.VMEM((w, 2 * w), F32),
    ]


PARAMS = pltpu.CompilerParams(vmem_limit_bytes=20 << 20)


def swaps(x, by, for_odd=None):
    size = lax.axis_size("slab")
    even, odd = [], []
    for i in range(size - by):
        pairs = odd if i // by % 2 else even
        pairs += [(i, i + by), (i + by, i)]
    from_odd = lax.ppermute(x if for_odd is None else for_odd, "slab", odd)
    from_even = lax.ppermute(x, "slab", even)
    return from_even, from_odd


def reduce_levels(onsite, hop, energy_level, broadening):
    rows, _, w, _ = onsite.shape
    onsite = onsite.reshape(rows, 2 * w, w)
    hop = hop.reshape(rows, 2 * w, w)
    last = lax.axis_index("slab") == lax.axis_size("slab") - 1
    keep = jnp.where(last, 0.0, 1.0).astype(F32)
    scalars = jnp.stack([energy_level[0], broadening[0], keep])
    position = lax.axis_index("slab")
    near, far = position & 1, (position >> 1) & 1
    at_a, at_b = (jnp.stack([near, far, slab]) for slab in (near, 1 - near))
    run_a, run_b = (
        jnp.stack([jnp.int32(run), side]) for run, side in ((0, 1 - near), (1, near))
    )
    scalars, at_a, at_b, run_a, run_b = lax.optimization_barrier(
        (scalars, at_a, at_b, run_a, run_b)
    )

    hop_even, hop_odd = swaps(hop, 1)
    block, pair, two = shape(2 * w, w), shape(4 * w, w), shape(2, 2 * w, w)
    z_even, z_odd, z_own = pl.pallas_call(
        first_kernel,
        out_shape=(block, block, two),
        in_specs=[VMEM, SMEM, SMEM],
        out_specs=(VMEM,) * 3,
        scratch_shapes=work(rows, w),
        compiler_params=PARAMS,
        name="first",
    )(onsite, scalars, at_a)
    from_even, from_odd = swaps(z_even, 1, z_odd)
    kept = pl.BlockSpec(memory_space=pl.ANY)
    gain = jax.ShapeDtypeStruct((2, 4, w, 2 * w), BF)
    d_near, c_near, g_near, k_near, d_out, u_out, l_out = pl.pallas_call(
        near_kernel,
        out_shape=(two, two, gain, two) + (two,) * 3,
        in_specs=[VMEM] * 5 + [SMEM] * 2,
        out_specs=(VMEM,) * 4 + (kept,) * 3,
        compiler_params=PARAMS,
        name="near",
    )(onsite, hop, hop_even, hop_odd, z_own, scalars, at_a)
    whole = two

    second = pl.pallas_call(
        second_kernel,
        out_shape=(block, two, pair),
        in_specs=[VMEM] * 5 + [SMEM] * 2,
        out_specs=(VMEM,) * 3,
        scratch_shapes=work(1, w),
        compiler_params=PARAMS,
        name="second",
    )
    d_b, c_b, p_a = second(d_near, c_near, g_near, from_even, k_near, scalars, run_a)
    even_a, odd_a = swaps(p_a, 1)
    d_a, c_a, p_b = second(d_near, c_near, g_near, from_odd, k_near, scalars, run_b)
    even_b, odd_b = swaps(p_b, 1)

    third = pl.pallas_call(
        third_kernel,
        out_shape=(block, two, pair),
        in_specs=[VMEM] * 4 + [SMEM] * 2,
        out_specs=(VMEM,) * 3,
        scratch_shapes=work(1, w),
        compiler_params=PARAMS,
        name="third",
    )
    d_a, c_a, p_a = third(d_a, c_a, even_a, odd_a, scalars, at_a)
    even_a, odd_a = swaps(p_a, 2)
    d_b, c_b, p_b = third(d_b, c_b, even_b, odd_b, scalars, at_a)
    first_b = swaps(p_b[: 2 * w], 2)
    cuts = (0, w // 2)
    lower_b = [swaps(p_b[2 * w :, cut : cut + w // 2], 2) for cut in cuts]

    def hold(wide):
        return [pltpu.VMEM((2, 2 * w, wide), F32), pltpu.SemaphoreType.DMA((2,))]

    take_upper = pl.pallas_call(
        functools.partial(last_kernel, 0, 0),
        out_shape=(block, whole),
        in_specs=[VMEM] * 4 + [SMEM, kept],
        out_specs=(VMEM, kept),
        input_output_aliases={5: 1},
        scratch_shapes=hold(w),
        compiler_params=PARAMS,
        name="take_upper",
    )
    take_lower = [
        pl.pallas_call(
            functools.partial(last_kernel, 1, cut),
            out_shape=(whole, whole),
            in_specs=[VMEM] * 4 + [SMEM, kept, kept],
            out_specs=(kept, kept),
            input_output_aliases={5: 1, 6: 0},
            scratch_shapes=hold(w // 2),
            compiler_params=PARAMS,
        )
        for cut in cuts
    ]
    d_a, u_out = take_upper(d_a, c_a, even_a[: 2 * w], odd_a[: 2 * w], at_a, u_out)
    for take, cut in zip(take_lower, cuts):
        arrived = (x[2 * w :, cut : cut + w // 2] for x in (even_a, odd_a))
        d_out, l_out = take(d_a, c_a, *arrived, at_a, l_out, d_out)
    d_b, u_out = take_upper(d_b, c_b, *first_b, at_b, u_out)
    for take, arrived in zip(take_lower, lower_b):
        d_out, l_out = take(d_b, c_b, *arrived, at_b, l_out, d_out)
    return tuple(x.reshape(rows, 2, w, w) for x in (d_out, u_out, l_out))


def solution(mesh):
    placed = (P("slab", None, None, None), P("slab", None, None, None), P("energy"), P("energy"))
    out = P(("energy", "slab"), None, None, None)
    return jax.shard_map(
        reduce_levels, mesh=mesh, in_specs=placed, out_specs=(out, out, out), check_vma=False
    )
```

```python
import functools

import jax
import jax.numpy as jnp
from jax import lax
from jax.experimental import pallas as pl
from jax.experimental.pallas import tpu as pltpu
from jax.sharding import PartitionSpec as P


BF = jnp.bfloat16
F32 = jnp.float32
HIGHEST = lax.Precision.HIGHEST
CONVERGED = 0.985
TRUSTED = 0.012
VMEM = pl.BlockSpec(memory_space=pltpu.VMEM)
SMEM = pl.BlockSpec(memory_space=pltpu.SMEM)


def dot(a, b):
    return jnp.dot(a, b, preferred_element_type=F32)


def exact_dot(a, b):
    return jnp.dot(a, b, precision=HIGHEST, preferred_element_type=F32)


def row(c):
    h = c.shape[0] // 2
    return jnp.concatenate([c[:h], c[h:]], axis=1)


def put(out, r, at=0):
    h, w = r.shape[0], r.shape[1] // 2
    out[at : at + h] = r[:, :w]
    out[at + h : at + 2 * h] = r[:, w:]


def turned(r):
    w = r.shape[1] // 2
    return jnp.concatenate([-r[:, w:], r[:, :w]], axis=1)


def emb(r):
    return jnp.concatenate([r, turned(r)], axis=0)


def adjoint(r):
    w = r.shape[0]
    return jnp.concatenate([r[:, :w].T, -r[:, w:].T], axis=1)


def split(x):
    high = x.astype(BF)
    return high, (x - high.astype(F32)).astype(BF)


def product(a, b):
    return times(split(a), b)


def times(a, b):
    return multiply(a, split(b))


def multiply(a, b):
    a_high, a_low = a
    b_high, b_low = b
    e_high, e_low = emb(b_high), emb(b_low)
    return dot(a_high, e_high) + dot(a_high, e_low) + dot(a_low, e_high)


def unit(w):
    at = lax.broadcasted_iota(jnp.int32, (w, 2 * w), 0)
    return (at == lax.broadcasted_iota(jnp.int32, (w, 2 * w), 1)).astype(F32)


def invert(blocks, eta, work, side=()):
    z, ea, el, ex, full, spread, rest = work
    w = blocks[0].shape[0]
    one = unit(w)
    halves = [slice(k * w // 2, (k + 1) * w // 2) for k in range(2)]

    def place(i, x):
        ex[i, :w] = x
        ex[i, w:] = turned(x)

    norms, grams = [], []
    for i, a in enumerate(blocks):
        high, low = split(a)
        ea[i] = emb(high)
        el[i] = emb(low)
        ah = adjoint(high)
        gram = dot(ah, ea[i])
        size = jnp.sqrt(gram[:, :w] * gram[:, :w] + gram[:, w:] * gram[:, w:])
        norm = 1.02 * jnp.max(jnp.sum(size, axis=1))
        place(i, (ah.astype(F32) * (1.0 / norm)).astype(BF))
        norms.append(norm)
        grams.append(gram)
    largest = functools.reduce(jnp.maximum, norms)
    bound = jnp.maximum(0.9 * eta * eta / largest, 1e-10)

    def step(bound, piece=None, known=None):
        mu = 2.0 / (bound + 1.03)
        for i in range(len(blocks)):
            if known is None:
                errors = [(one[h] - mu * dot(ex[i, h], ea[i])).astype(BF) for h in halves]
            else:
                errors = [(one[h] - (mu / norms[i]) * known[i][h]).astype(BF) for h in halves]
            if piece is not None:
                piece()
            news = [
                (mu * (ex[i, h].astype(F32) + dot(e, ex[i]))).astype(BF)
                for h, e in zip(halves, errors)
            ]
            place(i, jnp.concatenate(news, axis=0))
        gap = 1.0 - mu * bound
        return 1.0 - gap * gap

    bound = step(bound, side[0] if side else None, grams)
    for piece in side[1:]:
        bound = step(bound, piece)
    lax.while_loop(lambda bound: bound < CONVERGED, step, bound)
    for i, a in enumerate(blocks):
        x = ex[i, :w]
        error = one - (dot(x, ea[i]) + dot(x, el[i]))
        z[i] = x.astype(F32) + dot(error.astype(BF), ex[i])
        left = jnp.sum(error * error)

        @pl.when(jnp.logical_not(left <= TRUSTED))
        def _():
            polish(a, norms[i], left, z, i, full, spread, rest)


def polish(a, norm, left, z, i, full, spread, rest):
    w = a.shape[0]
    high, wide = min(32, w), min(128, w)
    across = 2 * w // wide
    full[...] = emb(a)

    @pl.when(jnp.logical_not(left <= 0.25))
    def _():
        z[i] = adjoint(a) * (1.0 / norm)

    def cut(k):
        top, side = k // across * high, k % across * wide
        return (
            top,
            side,
            pl.ds(pl.multiple_of(top, high), high),
            pl.ds(pl.multiple_of(side, wide), wide),
        )

    def once(state):
        def residual(k, total):
            top, side, rows, cols = cut(k)
            at = lax.broadcasted_iota(jnp.int32, (high, wide), 0) + top
            to = lax.broadcasted_iota(jnp.int32, (high, wide), 1) + side
            part = jnp.where(at == to, 1.0, 0.0) - exact_dot(z[i, rows, :], full[:, cols])
            rest[rows, cols] = part
            return total + jnp.sum(part * part)

        tiles = w // high * across
        total = lax.fori_loop(0, tiles, residual, jnp.float32(0.0))
        spread[...] = emb(z[i])

        def correct(k, _):
            _, _, rows, cols = cut(k)
            z[i, rows, cols] += exact_dot(rest[rows, :], spread[:, cols])
            return 0

        lax.fori_loop(0, tiles, correct, 0)
        return state[0] + 1, total

    lax.while_loop(
        lambda state: (state[0] < 64) & jnp.logical_not(state[1] <= 1e-6),
        once,
        (0, jnp.float32(1.0)),
    )


def initial(onsite, scalars):
    w = onsite.shape[0]
    at = lax.broadcasted_iota(jnp.int32, (w, 2 * w), 0)
    to = lax.broadcasted_iota(jnp.int32, (w, 2 * w), 1)
    shift = jnp.where(at == to, scalars[0], jnp.where(at + w == to, scalars[1], 0.0))
    return shift - onsite


def deferred(out, k, a, b, sign):
    a_high, a_low = split(a)
    b_high, b_low = split(b)

    def lead():
        put(out.at[k], sign * dot(a_high, emb(b_high)))

    def middle():
        put(out.at[k], row(out[k]) + sign * dot(a_high, emb(b_low)))

    def trail():
        put(out.at[k], row(out[k]) + sign * dot(a_low, emb(b_high)))

    return lead, middle, trail


def paired(first, second):
    def piece():
        first()
        second()

    return piece


def solve(d, couplings, side, eta, payload, work):
    invert([d], eta, work, side)
    z = split(work[0][0])
    for k in range(2):
        put(payload, times(z, row(couplings[1 - k])), k * d.shape[1])


def part(payload, k):
    rows = 2 * payload.shape[1]
    return row(payload[pl.ds(pl.multiple_of(k * rows, rows), rows)])


def sides(parity):
    return 1 - parity, parity


def first_kernel(onsite, hop, scalars, ints, z_even, z_odd, z_own, hop_own, sem, *work):
    beside = pltpu.make_async_copy(hop, hop_own, sem)
    beside.start()
    invert([initial(row(onsite[i]), scalars) for i in range(2)], scalars[1], work)
    for i in range(2):
        put(z_own.at[i], work[0][i])
    put(z_even, work[0][1 - ints[0]])
    put(z_odd, work[0][ints[0]])
    beside.wait()


def near_kernel(
    onsite, hop, hop_even, hop_odd, z, scalars, ints, d_out, c_out, g_out, k_out, *outputs
):
    run_b = ints[0]
    run_a = 1 - run_b
    left = [jnp.where(run_b == 0, hop_odd[k], hop_even[k]) for k in range(2)]
    right = jnp.where(run_b == 0, hop_even[0], hop_odd[0])
    h = row(hop[0])
    h_adj = adjoint(h)
    before, after = row(left[1]), row(hop[1])
    before_adj = adjoint(before)
    for run, pair in ((run_a, (before_adj, before)), (run_b, (after, adjoint(after)))):
        for k, value in enumerate(pair):
            high, low = split(value)
            g_out[run, 2 * k] = high
            g_out[run, 2 * k + 1] = low
    put(k_out.at[run_a], adjoint(row(left[0])))
    k_out[run_b] = right
    t = product(h, row(z[1]))
    put(d_out.at[run_a], initial(row(onsite[0]), scalars) - product(t, h_adj))
    put(c_out.at[run_a], product(t, after) * (-scalars[2]))
    t = product(h_adj, row(z[0]))
    put(d_out.at[run_b], initial(row(onsite[1]), scalars) - product(t, h))
    put(c_out.at[run_b], -product(t, before_adj))


def second_kernel(d_in, c_in, g, z, k, scalars, ints, d_out, c_out, payload, *work):
    run, at = ints[0], ints[1]
    t = times((g[run, 0], g[run, 1]), row(z[...]))
    put(d_out, row(d_in[run]) - multiply(split(t), (g[run, 2], g[run, 3])))
    c_out[1 - at] = c_in[run]
    pieces = deferred(c_out, at, t, row(k[run]), -1.0)
    solve(row(d_out[...]), c_out, pieces, scalars[1], payload, work)


def third_kernel(d_in, c_in, even, odd, scalars, parity, d_out, c_out, payload, *work):
    i, j = sides(parity[0])
    one, two = row(c_in[i]), row(c_in[j])
    d = row(d_in[...]) - product(one, part(even, i)) - product(two, part(odd, j))
    put(d_out, d)
    set_one = deferred(c_out, i, one, part(even, 1 - i), -1.0)
    set_two = deferred(c_out, j, two, part(odd, 1 - j), -1.0)
    side = [paired(*pair) for pair in zip(set_one, set_two)]
    solve(row(d_out[...]), c_out, side, scalars[1], payload, work)


def last_kernel(k, start, d_in, c_in, even, odd, ints, c_old, *refs):
    d_out, c_out = refs[-4:-2]
    hold, sems = refs[-2:]
    slab = ints[2]
    wide = even.shape[1]
    cols = pl.ds(start, wide)
    is_even = sides(ints[1])[0] == k
    to_d = row(jnp.where(is_even, even[...], odd[...]))
    to_c = row(jnp.where(is_even, odd[...], even[...]))
    put(hold.at[0], -product(row(c_in[1 - k]), to_c))
    copies = [pltpu.make_async_copy(hold.at[0], c_out.at[slab, :, cols], sems.at[0])]
    copies[0].start()
    d = row(d_in[:, start : start + wide]) - product(row(c_in[k]), to_d)
    if k == 0:
        put(d_out, d)
    else:
        put(hold.at[1], d)
        copies.append(pltpu.make_async_copy(hold.at[1], d_out.at[slab, :, cols], sems.at[1]))
        copies[1].start()
    for copy in copies:
        copy.wait()


def shape(*dims):
    return jax.ShapeDtypeStruct(dims, F32)


def work(count, w):
    return [
        pltpu.VMEM((count, w, 2 * w), F32),
        pltpu.VMEM((count, 2 * w, 2 * w), BF),
        pltpu.VMEM((count, 2 * w, 2 * w), BF),
        pltpu.VMEM((count, 2 * w, 2 * w), BF),
        pltpu.VMEM((2 * w, 2 * w), F32),
        pltpu.VMEM((2 * w, 2 * w), F32),
        pltpu.VMEM((w, 2 * w), F32),
    ]


PARAMS = pltpu.CompilerParams(vmem_limit_bytes=20 << 20)


def swaps(x, by, for_odd=None):
    size = lax.axis_size("slab")
    even, odd = [], []
    for i in range(size - by):
        pairs = odd if i // by % 2 else even
        pairs += [(i, i + by), (i + by, i)]
    from_odd = lax.ppermute(x if for_odd is None else for_odd, "slab", odd)
    from_even = lax.ppermute(x, "slab", even)
    return from_even, from_odd


def reduce_levels(onsite, hop, energy_level, broadening):
    rows, _, w, _ = onsite.shape
    onsite = onsite.reshape(rows, 2 * w, w)
    hop = hop.reshape(rows, 2 * w, w)
    last = lax.axis_index("slab") == lax.axis_size("slab") - 1
    keep = jnp.where(last, 0.0, 1.0).astype(F32)
    scalars = jnp.stack([energy_level[0], broadening[0], keep])
    position = lax.axis_index("slab")
    near, far = position & 1, (position >> 1) & 1
    at_a, at_b = (jnp.stack([near, far, slab]) for slab in (near, 1 - near))
    run_a, run_b = (
        jnp.stack([jnp.int32(run), side]) for run, side in ((0, 1 - near), (1, near))
    )
    scalars, at_a, at_b, run_a, run_b = lax.optimization_barrier(
        (scalars, at_a, at_b, run_a, run_b)
    )

    hop_even, hop_odd = swaps(hop, 1)
    block, pair, two = shape(2 * w, w), shape(4 * w, w), shape(2, 2 * w, w)
    z_even, z_odd, z_own, hop_own = pl.pallas_call(
        first_kernel,
        out_shape=(block, block, two, two),
        in_specs=[VMEM, pl.BlockSpec(memory_space=pl.ANY), SMEM, SMEM],
        out_specs=(VMEM,) * 4,
        scratch_shapes=[pltpu.SemaphoreType.DMA] + work(rows, w),
        compiler_params=PARAMS,
        name="first",
    )(onsite, pltpu.with_memory_space_constraint(hop, pltpu.HBM), scalars, at_a)
    from_even, from_odd = swaps(z_even, 1, z_odd)
    kept = pl.BlockSpec(memory_space=pl.ANY)
    gain = jax.ShapeDtypeStruct((2, 4, w, 2 * w), BF)
    d_near, c_near, g_near, k_near, d_out, u_out, l_out = pl.pallas_call(
        near_kernel,
        out_shape=(two, two, gain, two) + (two,) * 3,
        in_specs=[VMEM] * 5 + [SMEM] * 2,
        out_specs=(VMEM,) * 4 + (kept,) * 3,
        compiler_params=PARAMS,
        name="near",
    )(onsite, hop_own, hop_even, hop_odd, z_own, scalars, at_a)
    whole = two

    second = pl.pallas_call(
        second_kernel,
        out_shape=(block, two, pair),
        in_specs=[VMEM] * 5 + [SMEM] * 2,
        out_specs=(VMEM,) * 3,
        scratch_shapes=work(1, w),
        compiler_params=PARAMS,
        name="second",
    )
    d_b, c_b, p_a = second(d_near, c_near, g_near, from_even, k_near, scalars, run_a)
    even_a, odd_a = swaps(p_a, 1)
    d_a, c_a, p_b = second(d_near, c_near, g_near, from_odd, k_near, scalars, run_b)
    even_b, odd_b = swaps(p_b, 1)

    third = pl.pallas_call(
        third_kernel,
        out_shape=(block, two, pair),
        in_specs=[VMEM] * 4 + [SMEM] * 2,
        out_specs=(VMEM,) * 3,
        scratch_shapes=work(1, w),
        compiler_params=PARAMS,
        name="third",
    )
    d_a, c_a, p_a = third(d_a, c_a, even_a, odd_a, scalars, at_a)
    even_a, odd_a = swaps(p_a, 2)
    d_b, c_b, p_b = third(d_b, c_b, even_b, odd_b, scalars, at_a)
    first_b = swaps(p_b[: 2 * w], 2)
    cuts = (0, w // 2)
    lower_b = [swaps(p_b[2 * w :, cut : cut + w // 2], 2) for cut in cuts]

    def hold(wide):
        return [pltpu.VMEM((2, 2 * w, wide), F32), pltpu.SemaphoreType.DMA((2,))]

    take_upper = pl.pallas_call(
        functools.partial(last_kernel, 0, 0),
        out_shape=(block, whole),
        in_specs=[VMEM] * 4 + [SMEM, kept],
        out_specs=(VMEM, kept),
        input_output_aliases={5: 1},
        scratch_shapes=hold(w),
        compiler_params=PARAMS,
        name="take_upper",
    )
    take_lower = [
        pl.pallas_call(
            functools.partial(last_kernel, 1, cut),
            out_shape=(whole, whole),
            in_specs=[VMEM] * 4 + [SMEM, kept, kept],
            out_specs=(kept, kept),
            input_output_aliases={5: 1, 6: 0},
            scratch_shapes=hold(w // 2),
            compiler_params=PARAMS,
        )
        for cut in cuts
    ]
    d_a, u_out = take_upper(d_a, c_a, even_a[: 2 * w], odd_a[: 2 * w], at_a, u_out)
    for take, cut in zip(take_lower, cuts):
        arrived = (x[2 * w :, cut : cut + w // 2] for x in (even_a, odd_a))
        d_out, l_out = take(d_a, c_a, *arrived, at_a, l_out, d_out)
    d_b, u_out = take_upper(d_b, c_b, *first_b, at_b, u_out)
    for take, arrived in zip(take_lower, lower_b):
        d_out, l_out = take(d_b, c_b, *arrived, at_b, l_out, d_out)
    return tuple(x.reshape(rows, 2, w, w) for x in (d_out, u_out, l_out))


def solution(mesh):
    placed = (P("slab", None, None, None), P("slab", None, None, None), P("energy"), P("energy"))
    out = P(("energy", "slab"), None, None, None)
    return jax.shard_map(
        reduce_levels, mesh=mesh, in_specs=placed, out_specs=(out, out, out), check_vma=False
    )
```
